256 devices in a mesh: req: 32 (over x, y, core), tp: 8 (over z).
Axes of the slice: x: 4, y: 4, z: 8, core: 2. Of those that a mesh axis runs over, the one named last changes fastest.
Arguments:
- activations: bfloat16 [4096, 2560], P('req', 'tp'), may hold values from -12 to 12
- norm_gain: float32 [2560], replicated, may hold values from 0.1 to 1.9
- input_proj: bfloat16 [2560, 8, 480], P(None, 'tp'), may hold values from -0.125 to 0.125
- output_proj: bfloat16 [2560, 2560], P('tp'), may hold values from -0.125 to 0.125
- cache_pool: bfloat16 [3008, 8, 20480], P('req', 'tp'), may hold values from -103 to 103
- page_table: int32 [64, 32], replicated, may hold values from 0 to 93, as said below
- rebalance_plan: int32 [64, 32], replicated, may hold values from 0 to 31, as said below
- cached_lengths: int32 [64], replicated, may hold values from 1 to 4096, as said below
- token_positions: int32 [64, 64], replicated, may hold values from 1 to 4159, as said below
Outputs:
- attention_out: float32 [4096, 2560], P('req', 'tp')
The draws below stay inside these ranges and needn't reach their ends.
Inputs may be any that keep to these rules, and one draw needn't show every extreme that they name: token_positions[r, t] = cached_lengths[r] + t. `cached_lengths`: cached tokens of request r before its new ones; in every draw all requests of some group have 4096. rebalance_plan[r, j] is the request's own group for j < 16 and another group for later pages; page 16 of the first request of group q lies in group (q + 16) % 32; at most 2 of the pages j >= 16 of one group's requests lie in any one other group, and some group receives 2 from one other group in every draw. `page_table`: slot of page j of request r in the pool of group rebalance_plan[r, j]; no two entries of the table name the same group and slot.
All inputs are finite; a program needn't handle non-finite values.
Results may differ from the reference program's by a relative error of at most 0.0095.
The reference program's roundings to bfloat16 on the way count: a program that leaves them out, or rounds other values in their place, can miss the bound.
Values may be sent and summed in bfloat16 or wider, within the bound.
A program may use at most 128 MiB of HBM per device.

```python
import math
import jax
import jax.numpy as jnp
from jax import lax

D = 2560
H = 32
KVH = 8
HD = 80
WINDOW = 4096
PAGE = 128
KEEP = 16
NEW = 64
REQ_DEV = 2
G = 4
MAXP = 32
TAIL = 16
POOL_DEV = 94
SLOTS = 3008
REQUESTS = 64
TOKENS = 4096


def lengths_of(key):
    key_span, key_part, key_heavy = jax.random.split(jax.random.fold_in(key, 3), 3)
    group_count = REQUESTS // REQ_DEV
    span_draw = jax.random.randint(key_span, (REQUESTS,), 0, WINDOW)
    divisor = jax.random.randint(key_part, (REQUESTS,), 1, 3)
    drawn = 1 + span_draw // divisor
    heavy_group = jax.random.randint(key_heavy, (), 0, group_count)
    request_ids = jnp.arange(REQUESTS)
    drawn = jnp.where(request_ids // REQ_DEV == heavy_group, WINDOW, drawn)
    drawn = jnp.where(request_ids == (heavy_group + 1) % group_count * REQ_DEV, 1, drawn)
    return drawn.astype(jnp.int32)


def layout_of(key):
    key_owner, key_pool = jax.random.split(jax.random.fold_in(key, 5))
    group_count = REQUESTS // REQ_DEV
    others = group_count - 1
    entries = REQ_DEV * TAIL
    capacity = (entries + others - 1) // others

    def permute_others(sub_key):
        return jax.random.permutation(sub_key, others)

    def permute_pool(sub_key):
        return jax.random.permutation(sub_key, POOL_DEV)
    raw_offsets = jax.vmap(permute_others)(jax.random.split(key_owner, group_count))
    far_offset = group_count // 2 - 1
    offsets = (raw_offsets - raw_offsets[:, :1] + far_offset) % others
    entry_ids = jnp.arange(entries)
    offset_drawn = offsets[:, entry_ids % others]
    owners = jnp.arange(group_count)[:, None]
    holders = (owners + 1 + offset_drawn) % group_count
    tail_base = REQ_DEV * KEEP + offset_drawn * capacity + (entry_ids // others)[None, :]
    home_base = jnp.broadcast_to(jnp.arange(REQ_DEV * KEEP)[None, :], (group_count, REQ_DEV * KEEP))
    shuffles = jax.vmap(permute_pool)(jax.random.split(key_pool, group_count))
    home_slots = jnp.take_along_axis(shuffles, home_base, axis=1)
    tail_slots = shuffles[holders, tail_base]
    home_groups = jnp.broadcast_to(owners[:, :, None], (group_count, REQ_DEV, KEEP))
    plan_out = jnp.concatenate([home_groups, holders.reshape(group_count, REQ_DEV, TAIL)], axis=2)
    table_out = jnp.concatenate([home_slots.reshape(group_count, REQ_DEV, KEEP), tail_slots.reshape(group_count, REQ_DEV, TAIL)], axis=2)
    return (plan_out.reshape(REQUESTS, MAXP).astype(jnp.int32), table_out.reshape(REQUESTS, MAXP).astype(jnp.int32))


def draw_cached_lengths(key, part):
    return lengths_of(key)


def draw_token_positions(key, part):
    drawn = lengths_of(key)
    return (drawn[:, None] + jnp.arange(NEW)[None, :]).astype(jnp.int32)


def draw_rebalance_plan(key, part):
    return layout_of(key)[0]


def draw_page_table(key, part):
    return layout_of(key)[1]


def draw_activations(key, part):
    key_base, key_scale = jax.random.split(jax.random.fold_in(key, 11))
    base_draw = jax.random.truncated_normal(key_base, -4.0, 4.0, (TOKENS, D), jnp.float32)
    row_scale = jnp.exp(jax.random.uniform(key_scale, (TOKENS, 1), jnp.float32, math.log(0.3), math.log(3.0)))
    return (base_draw * row_scale).astype(jnp.bfloat16)


def draw_cache_pool(key, part):
    key_base = jax.random.fold_in(jax.random.fold_in(key, 13), 0)
    pool_shape = (SLOTS, KVH, PAGE, 2, HD)
    is_key = jnp.arange(2)[None, None, None, :, None] == 0
    base_draw = jax.random.truncated_normal(key_base, -4.0, 4.0, pool_shape, jnp.float32)
    factor = jnp.where(is_key, 1.5, 1.0)
    return (base_draw * factor).reshape(SLOTS, KVH, PAGE * 2 * HD).astype(jnp.bfloat16)


def block_scale(rng, extent, shards, low, top_value):
    def one(dim, shards_of):
        draws = jax.random.uniform(jax.random.fold_in(jax.random.fold_in(rng, 6), dim), (shards_of,), jnp.float32, low / len(shards), top_value / len(shards))
        return jnp.repeat(jnp.exp(draws), extent[dim] // shards_of).reshape((-1,) + (1,) * (len(extent) - dim - 1))

    loudness = one(*shards[0])
    for cut in shards[1:]:
        loudness = loudness * one(*cut)
    return loudness


def bell_draw(stream_key, dims, spread, bound, shards=(), kind=jnp.bfloat16):
    values = spread * jax.random.normal(stream_key, dims, jnp.float32)
    if shards:
        values = values * block_scale(stream_key, dims, shards, -0.22, 0.18)
    return jnp.clip(values, -bound, bound).astype(kind)


def setup_inputs(seed: int = 0) -> dict:
    arg_keys = jax.random.split(jax.random.key(seed), 10)
    return {
        "activations": draw_activations(jax.random.fold_in(arg_keys[9], 71), 0),
        "norm_gain": jnp.clip(1.0 + 0.18 * jax.random.normal(arg_keys[1], (D,), jnp.float32), 0.1, 1.9),
        "input_proj": bell_draw(arg_keys[2], (D, KVH, (G + 2) * HD), D ** -0.5, 0.125, ((1, 8),)),
        "output_proj": bell_draw(arg_keys[3], (H * HD, D), (H * HD) ** -0.5, 0.125, ((0, 8),)),
        "cache_pool": draw_cache_pool(jax.random.fold_in(arg_keys[9], 71), 0),
        "page_table": draw_page_table(jax.random.fold_in(arg_keys[9], 71), 0),
        "rebalance_plan": draw_rebalance_plan(jax.random.fold_in(arg_keys[9], 71), 0),
        "cached_lengths": draw_cached_lengths(jax.random.fold_in(arg_keys[9], 71), 0),
        "token_positions": draw_token_positions(jax.random.fold_in(arg_keys[9], 71), 0),
    }


EPSILON = 1e-05
THETA = 10000.0
MASKED = -1e+30

def rotate(values, places):
    half_dim = values.shape[-1] // 2
    frequency = THETA ** (-(jnp.arange(half_dim, dtype=jnp.float32) * 2.0 / values.shape[-1]))
    angles = places.astype(jnp.float32)[..., None] * frequency
    cosine = jnp.cos(angles)
    sine_part = jnp.sin(angles)
    front_half = values[..., :half_dim]
    back_half = values[..., half_dim:]
    return jnp.concatenate([front_half * cosine - back_half * sine_part, back_half * cosine + front_half * sine_part], axis=-1)

def reference(activations, norm_gain, input_proj, output_proj, cache_pool, page_table, rebalance_plan, cached_lengths, token_positions):
    scale_factor = HD ** (-0.5)
    group_size = H // KVH
    widened = activations.astype(jnp.float32)
    mean_square = lax.optimization_barrier(jnp.mean(widened * widened, axis=-1, keepdims=True))
    normed = (widened * lax.rsqrt(mean_square + EPSILON) * norm_gain).astype(jnp.bfloat16)
    projected = jnp.dot(normed, input_proj.reshape(D, KVH * (group_size + 2) * HD), preferred_element_type=jnp.float32)
    projected = projected.reshape(TOKENS, KVH, group_size + 2, HD)
    flat_places = token_positions.reshape(TOKENS)
    queries = rotate(projected[:, :, :group_size], jnp.broadcast_to(flat_places[:, None, None], (TOKENS, KVH, group_size))).astype(jnp.bfloat16)
    new_keys = rotate(projected[:, :, group_size], jnp.broadcast_to(flat_places[:, None], (TOKENS, KVH))).astype(jnp.bfloat16)
    new_values = projected[:, :, group_size + 1].astype(jnp.bfloat16)
    pool_view = cache_pool.reshape(SLOTS, KVH, PAGE, 2, HD)
    global_slot = rebalance_plan * POOL_DEV + page_table
    key_pos = jnp.arange(MAXP, dtype=jnp.int32)[:, None] * PAGE + jnp.arange(PAGE, dtype=jnp.int32)[None, :]
    causal = jnp.arange(NEW, dtype=jnp.int32)[:, None] >= jnp.arange(NEW, dtype=jnp.int32)[None, :]

    def one_request(request):
        page_data = pool_view[global_slot[request]]
        cache_keys = page_data[:, :, :, 0].astype(jnp.float32)
        cache_values = page_data[:, :, :, 1].astype(jnp.float32)
        first_row = (request * NEW).astype(jnp.int32)
        query_rows = lax.dynamic_slice_in_dim(queries, first_row, NEW, 0).astype(jnp.float32)
        key_rows = lax.dynamic_slice_in_dim(new_keys, first_row, NEW, 0).astype(jnp.float32)
        value_rows = lax.dynamic_slice_in_dim(new_values, first_row, NEW, 0).astype(jnp.float32)
        length = cached_lengths[request]
        places = token_positions[request]
        valid = (key_pos[None] < length) & (places[:, None, None] - key_pos[None] < WINDOW)
        valid_mask = valid[None, None]
        scores = jnp.einsum('tkgd,jkpd->kgtjp', query_rows, cache_keys) * scale_factor
        block_peaks = lax.optimization_barrier(jnp.max(jnp.where(valid_mask, scores, MASKED), axis=-1))
        rounded = lax.optimization_barrier(jnp.where(valid_mask, jnp.exp(scores - block_peaks[..., None]), 0.0).astype(jnp.bfloat16))
        probabilities = rounded.astype(jnp.float32)
        totals = lax.optimization_barrier(jnp.sum(probabilities, axis=-1))
        value_sums = jnp.einsum('kgtjp,jkpd->kgtjd', probabilities, cache_values)
        new_scores = jnp.einsum('tkgd,ukd->kgtu', query_rows, key_rows) * scale_factor
        new_peak = lax.optimization_barrier(jnp.max(jnp.where(causal, new_scores, MASKED), axis=-1))
        new_rounded = lax.optimization_barrier(jnp.where(causal, jnp.exp(new_scores - new_peak[..., None]), 0.0).astype(jnp.bfloat16))
        new_probs = new_rounded.astype(jnp.float32)
        new_total = lax.optimization_barrier(jnp.sum(new_probs, axis=-1))
        new_sum = jnp.einsum('kgtu,ukd->kgtd', new_probs, value_rows)
        overall = jnp.maximum(lax.optimization_barrier(jnp.max(block_peaks, axis=-1)), new_peak)
        weights = jnp.exp(block_peaks - overall[..., None])
        new_weight = jnp.exp(new_peak - overall)
        numerator = lax.optimization_barrier(jnp.sum(weights[..., None] * value_sums, axis=3)) + new_weight[..., None] * new_sum
        denominator = lax.optimization_barrier(jnp.sum(weights * totals, axis=-1)) + new_weight * new_total
        result = numerator / denominator[..., None]
        return jnp.transpose(result, (2, 0, 1, 3)).reshape(NEW, H * HD)
    head_rows = lax.map(one_request, jnp.arange(REQUESTS, dtype=jnp.int32))
    head_rows = head_rows.reshape(TOKENS, H * HD).astype(jnp.bfloat16)
    return jnp.dot(head_rows, output_proj, preferred_element_type=jnp.float32)
```

```python
import functools

import jax
import jax.numpy as jnp
import numpy as np
from jax import lax
from jax.experimental import pallas as pl
from jax.experimental.pallas import tpu as pltpu
from jax.sharding import PartitionSpec as P

MESH = pl.DeviceIdType.MESH
HD = 80
HALF = 40
WINDOW = 4096
PAGE = 128
KEEP = 16
TAIL = 16
NEW = 64
G = 4
GROUPS = 32
TP = 8
POOL = 94
D = 2560
ROWS = 32
WIDTH = 640
XB = 320
EPSILON = 1e-05
LOG_THETA = 9.210340371976184
MASKED = -1e30
SCALE = HD ** (-0.5) * 1.4426950408889634
KEY_TILE = ((0, 128, 0), (128, 128, 32), (256, 256, 64), (384, 256, 96))
VAL_TILE = ((0, 256, 80), (128, 256, 112), (384, 128, 16), (512, 128, 48))
OFFSETS = [(x, y, c) for x in range(4) for y in range(4) for c in range(2) if (x, y, c) != (0, 0, 0)]
np.random.RandomState(0).shuffle(OFFSETS)


STATED = (2, 0, 0)


def mm(a, b, contract):
    return lax.dot_general(a, b, (contract, ((), ())), preferred_element_type=jnp.float32)


def iota(shape, dim):
    return lax.broadcasted_iota(jnp.int32, shape, dim)


def kernel(
    rounds,
    x_hbm, gain_ref, w_hbm, wo_hbm, pool_hbm, table_ref, plan_ref, lens_ref, lens_s,
    out_ref,
    xf, pool, w, gb, wo, wot, gs, send, recv, xh, xt, qs, kn, vn, sc, stat, acc, hs, ht, rsend, rrecv, idx_v, idx,
    load_sem, page_ss, page_rs, ag_ss, ag_rs, rs_ss, rs_rs,
):
    me = lax.axis_index("req")
    z = lax.axis_index("tp")
    mx, my, mc = me // 8, (me // 2) % 4, me % 2
    zr, zl = lax.rem(z + 1, TP), lax.rem(z + TP - 1, TP)
    f32, bf16 = jnp.float32, jnp.bfloat16

    def peer(o):
        return ((mx + o[0]) % 4) * 8 + ((my + o[1]) % 4) * 2 + (mc + o[2]) % 2

    own = pl.ds(pl.multiple_of(z * XB, 64), XB)
    loads = [
        pltpu.make_async_copy(x_hbm, xf.at[own], load_sem.at[0]),
        pltpu.make_async_copy(pool_hbm, pool, load_sem.at[1]),
        pltpu.make_async_copy(w_hbm, w, load_sem.at[2]),
        pltpu.make_async_copy(wo_hbm, wo, load_sem.at[3]),
    ]
    for c in loads:
        c.start()
    barrier = pltpu.get_barrier_semaphore()
    for o in OFFSETS:
        pl.semaphore_signal(barrier, inc=1, device_id={"req": peer(o)}, device_id_type=MESH)
    for n in (zl, zr):
        pl.semaphore_signal(barrier, inc=1, device_id={"tp": n}, device_id_type=MESH)

    plan = plan_ref[KEEP:, :]
    table = table_ref[KEEP:, :]
    page_pos = (iota((TAIL, 64), 0) + KEEP) * PAGE
    held = (plan == me) & (page_pos < lens_ref[...])
    held_f = held.astype(f32)
    below = (iota((TAIL, TAIL), 0) > iota((TAIL, TAIL), 1)).astype(f32)
    rank = mm(below, held_f, ((1,), (0,)))
    count = mm(jnp.ones((8, TAIL), f32), held_f, ((1,), (0,)))
    r0, r1 = iota((64, 64), 0), iota((64, 64), 1)
    before = ((r1 % 2 == 1) & (r0 == r1 - 1)).astype(f32)
    rank = rank + mm(count, before, ((1,), (0,)))[0:1, :]
    slot_f = (table + 1).astype(f32)
    pair = (iota((GROUPS, 64), 0) == iota((GROUPS, 64), 1) // 2).astype(f32)
    sels = []
    for c in range(2):
        value = jnp.where(held & (rank == c), slot_f, 0.0)
        by_req = mm(value, jnp.ones((TAIL, 128), f32), ((0,), (0,)))
        col = mm(pair, by_req, ((1,), (0,)))[:, :POOL]
        sels.append((col == (iota((GROUPS, POOL), 1) + 1).astype(f32)).astype(bf16))
    tab = table_ref[:KEEP, :].astype(f32)
    lane = iota((KEEP, 64), 1)
    for a in range(2):
        col = jnp.sum(jnp.where(lane == 2 * me + a, tab, 0.0), axis=1, keepdims=True)
        sels.append((col == iota((KEEP, POOL), 1).astype(f32)).astype(bf16))
    sel = jnp.concatenate(sels, axis=0)

    loads[0].wait()
    pl.semaphore_wait(barrier, len(OFFSETS) + 2)

    def ag(step, way):
        block = lax.rem(z - step + TP, TP) if way == 0 else lax.rem(z + step, TP)
        rows = pl.ds(pl.multiple_of(block * XB, 64), XB)
        return pltpu.make_async_remote_copy(
            src_ref=xf.at[rows], dst_ref=xf.at[rows],
            send_sem=ag_ss.at[way * 4 + step], recv_sem=ag_rs.at[way * 4 + step],
            device_id={"tp": zr if way == 0 else zl}, device_id_type=MESH,
        )

    ags = {}

    def ag_step(step):
        for way in range(2):
            if step:
                ags[step - 1, way].wait_recv()
            if way == 0 or step < 3:
                ags[step, way] = ag(step, way)
                ags[step, way].start()

    ag_step(0)
    loads[1].wait()

    def pick(n, carry):
        for u in range(4):
            i = n * 4 + u
            rows = mm(sel, pool[:, pl.ds(pl.multiple_of(i * WIDTH, 128), WIDTH)], ((1,), (0,)))
            for k in range(5):
                gs[k, pl.ds(pl.multiple_of(i * 64, 64), 64), :] = rows[:64, k * 128 : (k + 1) * 128]
            at = pl.ds(pl.multiple_of(i * KEEP, KEEP), KEEP)
            xh[0, at, :] = rows[64 : 64 + KEEP].astype(bf16)
            xh[1, at, :] = rows[64 + KEEP :].astype(bf16)
        return carry

    lax.fori_loop(0, ROWS // 4, pick, 0)
    ag_step(1)

    def slots(o):
        return 2 if rounds == 2 or o == STATED else 1

    copies = []
    for n, o in enumerate(OFFSETS):
        p = peer(o)
        for c in range(slots(o)):
            for k in range(5):
                send[p, c, :, k * 128 : (k + 1) * 128] = gs[k, pl.ds(c * GROUPS + p, ROWS, stride=64), :].astype(bf16)
        held_slots = pl.ds(0, slots(o))
        copy = pltpu.make_async_remote_copy(
            src_ref=send.at[p, held_slots], dst_ref=recv.at[me, held_slots],
            send_sem=page_ss.at[n], recv_sem=page_rs.at[n], device_id={"req": p}, device_id_type=MESH,
        )
        copy.start()
        copies.append(copy)
    ag_step(2)

    cols, oks = [], []
    for a in range(2):
        cols.append(jnp.sum(jnp.where(lane == 2 * me + a, plan.astype(f32), 0.0), axis=1, keepdims=True))
        inside = (page_pos < lens_ref[...]).astype(f32)
        oks.append(jnp.sum(jnp.where(lane == 2 * me + a, inside, 0.0), axis=1, keepdims=True))
    group_col, ok_col = jnp.concatenate(cols, axis=0), jnp.concatenate(oks, axis=0)
    e0, e1 = iota((2 * TAIL, 128), 0), iota((2 * TAIL, 128), 1)
    group_row = jnp.sum(jnp.where(e0 == e1, group_col, 0.0), axis=0, keepdims=True)
    ok_row = jnp.sum(jnp.where(e0 == e1, ok_col, 0.0), axis=0, keepdims=True)
    earlier = jnp.where((group_col == group_row) & (e0 < e1), ok_col, 0.0)
    where_row = group_row * 2.0 + ok_row * jnp.sum(earlier, axis=0, keepdims=True)
    idx_v[...] = jnp.broadcast_to(where_row, (8, 128)).astype(jnp.int32)
    idx_copy = pltpu.make_async_copy(idx_v, idx, load_sem.at[4])
    idx_copy.start()

    for i in range(20):
        gb[i * 128 : (i + 1) * 128, :] = jnp.transpose(jnp.broadcast_to(gain_ref[i : i + 1, :], (128, 128)))
    ag_step(3)
    loads[3].wait()
    for i in range(20):
        wot[i * 128 : (i + 1) * 128, :] = jnp.transpose(wo[:, i * 128 : (i + 1) * 128])
    loads[2].wait()
    ags[3, 0].wait_recv()

    xw = xf[...].astype(f32)
    rstd = lax.rsqrt(jnp.sum(xw * xw, axis=0, keepdims=True) * (1.0 / D) + EPSILON)
    normed = (xw * rstd * gb[...]).astype(bf16)
    proj = mm(w[...], normed, ((1,), (0,)))
    lens0, lens1 = lens_s[2 * me], lens_s[2 * me + 1]
    tok = iota((1, 2 * NEW), 1)
    places = jnp.where(tok < NEW, lens0 + tok, lens1 + tok - NEW).astype(f32)
    freq = jnp.exp(iota((HALF, 128), 0).astype(f32) * (-2.0 * LOG_THETA / HD))
    angle = freq * places
    cos, sin = jnp.cos(angle), jnp.sin(angle)

    def rotated(first):
        front, back = proj[first : first + HALF], proj[first + HALF : first + HD]
        full = jnp.concatenate([front * cos - back * sin, back * cos + front * sin], axis=0)
        return full.astype(bf16).astype(f32)

    def turned(values, offset, width):
        pieces = [values]
        if offset:
            pieces.insert(0, jnp.zeros((offset, 2 * NEW), f32))
        pieces.append(jnp.zeros((width - offset - HD, 2 * NEW), f32))
        return jnp.transpose(jnp.concatenate(pieces, axis=0)).astype(bf16)

    for g in range(G):
        q = rotated(g * HD)
        for m, (_, width, offset) in enumerate(KEY_TILE):
            qt = turned(q, offset, width)
            for a in range(2):
                qs[m, a, g * NEW : (g + 1) * NEW, :width] = qt[a * NEW : (a + 1) * NEW]
    kn[...] = turned(rotated(G * HD), 0, 128)
    vn[...] = turned(proj[(G + 1) * HD :].astype(bf16).astype(f32), 0, 128)

    t_col = iota((G * NEW, 1), 0) % NEW

    def attend(a, keys, pos_of, top0, with_window):
        length = lens_s[2 * me + a]
        cols = iota((1, 512), 1)
        top = top0
        for m, (first, width, _) in enumerate(KEY_TILE):
            s = mm(qs[m, a, :, :width], keys[:, first : first + width], ((1,), (1,)))
            rel = pos_of(cols) + m - length
            ok = rel < 0
            if with_window:
                ok = ok & (rel > t_col - WINDOW)
            s = jnp.where(ok, s, MASKED)
            sc[m] = s
            top = jnp.maximum(top, jnp.max(s, axis=1, keepdims=True))
        total = jnp.zeros((G * NEW, 1), f32)
        sums = jnp.zeros((G * NEW, 128), f32)
        for m, (first, width, offset) in enumerate(VAL_TILE):
            p = jnp.exp2((sc[m] - top) * SCALE)
            total = total + jnp.sum(p, axis=1, keepdims=True)
            o = mm(p.astype(bf16), keys[:, first : first + width], ((1,), (0,)))
            sums = sums + pltpu.roll(o, width - offset, 1)[:, :128]
        return top, total, sums

    def home(a, carry):
        at = pl.ds(pl.multiple_of(a * NEW, NEW), NEW)
        s = mm(qs[0, a, :, :128], kn[at, :], ((1,), (1,)))
        s = jnp.where(iota((G * NEW, NEW), 1) <= t_col, s, MASKED)
        top_new = jnp.max(s, axis=1, keepdims=True)
        top, total, sums = attend(
            a, xh.at[a], lambda col: (col % KEEP) * PAGE + (col // KEEP) * 4, top_new, True
        )
        p = jnp.exp2((s - top) * SCALE)
        stat[a, 0] = jnp.broadcast_to(top, (G * NEW, 128))
        stat[a, 1] = jnp.broadcast_to(total + jnp.sum(p, axis=1, keepdims=True), (G * NEW, 128))
        acc[a] = sums + mm(p.astype(bf16), vn[at, :], ((1,), (0,)))
        return carry

    lax.fori_loop(0, 2, home, 0)

    idx_copy.wait()
    for copy in copies:
        copy.wait_recv()

    def tail(a, carry):
        for j in range(TAIL):
            where = jnp.clip(idx[0, a * TAIL + j], 0, 2 * GROUPS - 1)
            xt[j * ROWS : (j + 1) * ROWS, :] = recv[where // 2, where % 2]
        old_top = stat[a, 0][:, :1]
        top, total, sums = attend(a, xt, lambda col: KEEP * PAGE + col * 4, old_top, False)
        weight = jnp.exp2((old_top - top) * SCALE)
        result = (acc[a] * weight + sums) / (stat[a, 1][:, :1] * weight + total)
        for g in range(G):
            hs[g, pl.ds(pl.multiple_of(a * NEW, NEW), NEW), :] = result[g * NEW : (g + 1) * NEW]
        return carry

    lax.fori_loop(0, 2, tail, 0)
    for g in range(G):
        ht[g * HD : (g + 1) * HD, :] = jnp.transpose(hs[g])[:HD].astype(bf16)

    def project(dest):
        rows = pl.ds(pl.multiple_of(dest * XB, 64), XB)
        return mm(wot[rows, :], ht[...], ((1,), (0,)))

    HB = XB // 2
    pending = {}
    for step in range(4):
        for way in range(2):
            hop = step if way == 0 else step - 1
            if hop < 0:
                continue
            dest = lax.rem(z + 4 - step, TP) if way == 0 else lax.rem(z + TP - 3 + hop, TP)
            mine = project(dest)
            for h in range(2):
                n = way * 8 + hop * 2 + h
                block = mine[h * HB : (h + 1) * HB]
                if hop:
                    pending[n - 2].wait_recv()
                    block = block + rrecv[n - 2].astype(f32)
                rsend[n] = block.astype(bf16)
                copy = pltpu.make_async_remote_copy(
                    src_ref=rsend.at[n], dst_ref=rrecv.at[n], send_sem=rs_ss.at[n], recv_sem=rs_rs.at[n],
                    device_id={"tp": zr if way == 0 else zl}, device_id_type=MESH,
                )
                copy.start()
                pending[n] = copy
    mine = project(z)
    for h in range(2):
        last = (6 + h, 8 + 4 + h)
        block = mine[h * HB : (h + 1) * HB]
        for n in last:
            pending[n].wait_recv()
            block = block + rrecv[n].astype(f32)
        out_ref[h * HB : (h + 1) * HB, :] = block

    for copy in list(ags.values()) + copies + list(pending.values()):
        copy.wait_send()


def second_round(plan_ref, lens_ref, out_ref):
    f32 = jnp.float32
    group = iota((GROUPS, 64), 0)
    held = jnp.zeros((GROUPS, 64), f32)
    for j in range(KEEP, KEEP + TAIL):
        held += ((plan_ref[j : j + 1, :] == group) & (lens_ref[...] > j * PAGE)).astype(f32)
    pair = (iota((64, GROUPS), 0) // 2 == iota((64, GROUPS), 1)).astype(f32)
    pages = mm(held, pair, ((1,), (0,)))
    r0, r1 = iota((GROUPS, GROUPS), 0), iota((GROUPS, GROUPS), 1)
    pages = jnp.where(r0 == (r1 + GROUPS // 2) % GROUPS, 0.0, pages)
    out_ref[0] = (jnp.max(pages) > 1.5).astype(jnp.int32)


def layer(rounds, *operands):
    any_space = pl.BlockSpec(memory_space=pl.ANY)
    vmem = pl.BlockSpec(memory_space=pltpu.VMEM)
    smem = pl.BlockSpec(memory_space=pltpu.SMEM)
    f32, bf16 = jnp.float32, jnp.bfloat16
    dma = pltpu.SemaphoreType.DMA
    return pl.pallas_call(
        functools.partial(kernel, rounds),
        out_shape=jax.ShapeDtypeStruct((XB, 128), f32),
        in_specs=[any_space, vmem, any_space, any_space, any_space, vmem, vmem, vmem, smem],
        out_specs=vmem,
        scratch_shapes=[
            pltpu.VMEM((D, 128), bf16),
            pltpu.VMEM((POOL, ROWS * WIDTH), bf16),
            pltpu.VMEM((480, D), bf16),
            pltpu.VMEM((D, 128), f32),
            pltpu.VMEM((XB, D), bf16),
            pltpu.VMEM((D, XB), bf16),
            pltpu.VMEM((5, ROWS * 64, 128), f32),
            pltpu.VMEM((GROUPS, 2, ROWS, WIDTH), bf16),
            pltpu.VMEM((GROUPS, 2, ROWS, WIDTH), bf16),
            pltpu.VMEM((2, 512, WIDTH), bf16),
            pltpu.VMEM((512, WIDTH), bf16),
            pltpu.VMEM((4, 2, G * NEW, 256), bf16),
            pltpu.VMEM((128, 128), bf16),
            pltpu.VMEM((128, 128), bf16),
            pltpu.VMEM((4, G * NEW, 512), f32),
            pltpu.VMEM((2, 2, G * NEW, 128), f32),
            pltpu.VMEM((2, G * NEW, 128), f32),
            pltpu.VMEM((G, 128, 128), f32),
            pltpu.VMEM((XB, 128), bf16),
            pltpu.VMEM((16, XB // 2, 128), bf16),
            pltpu.VMEM((16, XB // 2, 128), bf16),
            pltpu.VMEM((8, 128), jnp.int32),
            pltpu.SMEM((8, 128), jnp.int32),
            dma((5,)), dma((31,)), dma((31,)), dma((8,)), dma((8,)), dma((16,)), dma((16,)),
        ],
        compiler_params=pltpu.CompilerParams(
            collective_id=rounds, has_side_effects=True, vmem_limit_bytes=60 * 2**20
        ),
        name=f"paged_prefill_{rounds}",
    )(*operands)


def local(activations, norm_gain, input_proj, output_proj, cache_pool, page_table, rebalance_plan, cached_lengths, token_positions):
    vmem = pl.BlockSpec(memory_space=pltpu.VMEM)
    plan, lens = rebalance_plan.T, cached_lengths.reshape(1, 64)
    more = pl.pallas_call(
        second_round,
        out_shape=jax.ShapeDtypeStruct((1,), jnp.int32),
        in_specs=[vmem, vmem],
        out_specs=pl.BlockSpec(memory_space=pltpu.SMEM),
        name="second_round",
    )(plan, lens)
    out = lax.cond(
        more[0] > 0,
        functools.partial(layer, 2),
        functools.partial(layer, 1),
        activations.T,
        norm_gain.reshape(20, 128),
        jnp.transpose(input_proj, (1, 2, 0)).reshape(480, D),
        output_proj,
        cache_pool.reshape(POOL, ROWS * WIDTH),
        page_table.T,
        plan,
        lens,
        cached_lengths,
    )
    return out.T


def solution(mesh):
    in_specs = (
        P("req", "tp"), P(), P(None, "tp", None), P("tp", None), P("req", "tp", None), P(), P(), P(), P(),
    )
    return jax.shard_map(local, mesh=mesh, in_specs=in_specs, out_specs=P("req", "tp"), check_vma=False)
```

```python
import functools

import jax
import jax.numpy as jnp
from jax import lax
from jax.experimental import pallas as pl
from jax.experimental.pallas import tpu as pltpu
from jax.sharding import PartitionSpec as P

MESH = pl.DeviceIdType.MESH
HD = 80
HALF = 40
WINDOW = 4096
PAGE = 128
KEEP = 16
TAIL = 16
NEW = 64
G = 4
GROUPS = 32
TP = 8
POOL = 94
D = 2560
ROWS = 32
WIDTH = 640
XB = 320
EPSILON = 1e-05
LOG_THETA = 9.210340371976184
MASKED = -1e30
SCALE = HD ** (-0.5) * 1.4426950408889634
KEY_TILE = ((0, 128, 0), (128, 128, 32), (256, 256, 64), (384, 256, 96))
VAL_TILE = ((0, 256, 80), (128, 256, 112), (384, 128, 16), (512, 128, 48))
OFFSETS = [(x, y, c) for x in range(4) for y in range(4) for c in range(2) if (x, y, c) != (0, 0, 0)]
OFFSETS.sort(key=lambda o: -min(o[0], 4 - o[0]) - min(o[1], 4 - o[1]))
Z_STEPS = (4, 3, 5, 2, 6, 1, 7)
STATED = (2, 0, 0)


def mm(a, b, contract):
    return lax.dot_general(a, b, (contract, ((), ())), preferred_element_type=jnp.float32)


def iota(shape, dim):
    return lax.broadcasted_iota(jnp.int32, shape, dim)


def kernel(
    rounds,
    x_hbm, gain_ref, w_hbm, wo_hbm, pool_hbm, table_ref, plan_ref, lens_ref, lens_s,
    out_ref, more_ref,
    xf, pool, w, gb, wo, wot, gs, send, recv, xh, xt, qs, kn, vn, sc, stat, acc, hs, ht, rsend, rrecv, idx_v, idx,
    load_sem, page_ss, page_rs, ag_ss, ag_rs, rs_ss, rs_rs,
):
    me = lax.axis_index("req")
    z = lax.axis_index("tp")
    mx, my, mc = me // 8, (me // 2) % 4, me % 2
    f32, bf16 = jnp.float32, jnp.bfloat16

    def peer(o):
        return ((mx + o[0]) % 4) * 8 + ((my + o[1]) % 4) * 2 + (mc + o[2]) % 2

    own = pl.ds(pl.multiple_of(z * XB, 64), XB)
    loads = [
        pltpu.make_async_copy(x_hbm, xf.at[own], load_sem.at[0]),
        pltpu.make_async_copy(pool_hbm, pool, load_sem.at[1]),
        pltpu.make_async_copy(w_hbm, w, load_sem.at[2]),
        pltpu.make_async_copy(wo_hbm, wo, load_sem.at[3]),
    ]
    for c in loads:
        c.start()
    barrier = pltpu.get_barrier_semaphore()
    for o in OFFSETS:
        pl.semaphore_signal(barrier, inc=1, device_id={"req": peer(o)}, device_id_type=MESH)
    for k in Z_STEPS:
        pl.semaphore_signal(barrier, inc=1, device_id={"tp": lax.rem(z + k, TP)}, device_id_type=MESH)

    plan = plan_ref[KEEP:, :]
    table = table_ref[KEEP:, :]
    page_pos = (iota((TAIL, 64), 0) + KEEP) * PAGE
    held = (plan == me) & (page_pos < lens_ref[...])
    held_f = held.astype(f32)
    below = (iota((TAIL, TAIL), 0) > iota((TAIL, TAIL), 1)).astype(f32)
    rank = mm(below, held_f, ((1,), (0,)))
    count = mm(jnp.ones((8, TAIL), f32), held_f, ((1,), (0,)))
    r0, r1 = iota((64, 64), 0), iota((64, 64), 1)
    before = ((r1 % 2 == 1) & (r0 == r1 - 1)).astype(f32)
    rank = rank + mm(count, before, ((1,), (0,)))[0:1, :]
    slot_f = (table + 1).astype(f32)
    pair = (iota((GROUPS, 64), 0) == iota((GROUPS, 64), 1) // 2).astype(f32)
    stated = peer(STATED)
    sels = []
    for c in range(2):
        value = jnp.where(held & (rank == c), slot_f, 0.0)
        by_req = mm(value, jnp.ones((TAIL, 128), f32), ((0,), (0,)))
        col = mm(pair, by_req, ((1,), (0,)))[:, :POOL]
        if c == 1 and rounds == 1:
            col = jnp.sum(jnp.where(iota((GROUPS, POOL), 0) == stated, col, 0.0), axis=0, keepdims=True)
            col = jnp.broadcast_to(col, (8, POOL))
        sels.append((col == (iota(col.shape, 1) + 1).astype(f32)).astype(bf16))
    sel = jnp.concatenate(sels, axis=0)
    out_rows = sel.shape[0]

    loads[0].wait()
    pl.semaphore_wait(barrier, len(OFFSETS) + len(Z_STEPS))

    ags = []
    for k in Z_STEPS:
        copy = pltpu.make_async_remote_copy(
            src_ref=xf.at[own], dst_ref=xf.at[own], send_sem=ag_ss.at[k], recv_sem=ag_rs.at[k],
            device_id={"tp": lax.rem(z + k, TP)}, device_id_type=MESH,
        )
        copy.start()
        ags.append(copy)
    loads[1].wait()

    def slots(o):
        return 2 if rounds == 2 or o == STATED else 1

    copies = []
    half_rows = ROWS // 2
    for half in range(2):

        def pick(n, carry, half=half):
            for u in range(4):
                i = half * half_rows + n * 4 + u
                rows = mm(sel, pool[:, pl.ds(pl.multiple_of(i * WIDTH, 128), WIDTH)], ((1,), (0,)))
                for k in range(5):
                    gs[k, pl.ds(pl.multiple_of(i * out_rows, 8), out_rows), :] = rows[:, k * 128 : (k + 1) * 128]
            return carry

        lax.fori_loop(0, half_rows // 4, pick, 0)
        at = pl.ds(half * half_rows, half_rows)
        for n, o in enumerate(OFFSETS):
            p = peer(o)
            for c in range(slots(o)):
                row = half * half_rows * out_rows + c * GROUPS + (0 if c == 1 and rounds == 1 else p)
                for k in range(5):
                    send[p, c, at, k * 128 : (k + 1) * 128] = gs[
                        k, pl.ds(row, half_rows, stride=out_rows), :
                    ].astype(bf16)
            held_slots = pl.ds(0, slots(o))
            copy = pltpu.make_async_remote_copy(
                src_ref=send.at[p, held_slots, at], dst_ref=recv.at[me, held_slots, at],
                send_sem=page_ss.at[half, n], recv_sem=page_rs.at[half, n],
                device_id={"req": p}, device_id_type=MESH,
            )
            copy.start()
            copies.append(copy)

    tab = table_ref[:KEEP, :].astype(f32)
    lane = iota((KEEP, 64), 1)
    homes = []
    for a in range(2):
        col = jnp.sum(jnp.where(lane == 2 * me + a, tab, 0.0), axis=1, keepdims=True)
        homes.append((col == iota((KEEP, POOL), 1).astype(f32)).astype(bf16))
    home_sel = jnp.concatenate(homes, axis=0)

    def pick_home(n, carry):
        for u in range(4):
            i = n * 4 + u
            rows = mm(home_sel, pool[:, pl.ds(pl.multiple_of(i * WIDTH, 128), WIDTH)], ((1,), (0,))).astype(bf16)
            at = pl.ds(pl.multiple_of(i * KEEP, KEEP), KEEP)
            xh[0, at, :] = rows[:KEEP]
            xh[1, at, :] = rows[KEEP:]
        return carry

    lax.fori_loop(0, ROWS // 4, pick_home, 0)

    cols, oks = [], []
    for a in range(2):
        cols.append(jnp.sum(jnp.where(lane == 2 * me + a, plan.astype(f32), 0.0), axis=1, keepdims=True))
        inside = (page_pos < lens_ref[...]).astype(f32)
        oks.append(jnp.sum(jnp.where(lane == 2 * me + a, inside, 0.0), axis=1, keepdims=True))
    group_col, ok_col = jnp.concatenate(cols, axis=0), jnp.concatenate(oks, axis=0)
    e0, e1 = iota((2 * TAIL, 128), 0), iota((2 * TAIL, 128), 1)
    group_row = jnp.sum(jnp.where(e0 == e1, group_col, 0.0), axis=0, keepdims=True)
    ok_row = jnp.sum(jnp.where(e0 == e1, ok_col, 0.0), axis=0, keepdims=True)
    earlier = jnp.where((group_col == group_row) & (e0 < e1), ok_col, 0.0)
    where_row = group_row * 2.0 + ok_row * jnp.sum(earlier, axis=0, keepdims=True)
    idx_v[...] = jnp.broadcast_to(where_row, (8, 128)).astype(jnp.int32)
    idx_copy = pltpu.make_async_copy(idx_v, idx, load_sem.at[4])
    idx_copy.start()

    for i in range(20):
        gb[i * 128 : (i + 1) * 128, :] = jnp.transpose(jnp.broadcast_to(gain_ref[i : i + 1, :], (128, 128)))
    loads[3].wait()
    for i in range(20):
        wot[i * 128 : (i + 1) * 128, :] = jnp.transpose(wo[:, i * 128 : (i + 1) * 128])
    group = iota((GROUPS, 64), 0)
    owed = jnp.zeros((GROUPS, 64), f32)
    for j in range(KEEP, KEEP + TAIL):
        owed += ((plan_ref[j : j + 1, :] == group) & (lens_ref[...] > j * PAGE)).astype(f32)
    owed = mm(owed, (iota((64, GROUPS), 0) // 2 == iota((64, GROUPS), 1)).astype(f32), ((1,), (0,)))
    g0, g1 = iota((GROUPS, GROUPS), 0), iota((GROUPS, GROUPS), 1)
    owed = jnp.where(g0 == (g1 + GROUPS // 2) % GROUPS, 0.0, owed)
    more_ref[0] = (jnp.max(owed) > 1.5).astype(jnp.int32)

    loads[2].wait()
    for copy in ags:
        copy.wait_recv()

    xw = xf[...].astype(f32)
    rstd = lax.rsqrt(jnp.sum(xw * xw, axis=0, keepdims=True) * (1.0 / D) + EPSILON)
    normed = (xw * rstd * gb[...]).astype(bf16)
    proj = mm(w[...], normed, ((1,), (0,)))
    lens0, lens1 = lens_s[2 * me], lens_s[2 * me + 1]
    tok = iota((1, 2 * NEW), 1)
    places = jnp.where(tok < NEW, lens0 + tok, lens1 + tok - NEW).astype(f32)
    freq = jnp.exp(iota((HALF, 128), 0).astype(f32) * (-2.0 * LOG_THETA / HD))
    angle = freq * places
    cos, sin = jnp.cos(angle), jnp.sin(angle)

    def rotated(first):
        front, back = proj[first : first + HALF], proj[first + HALF : first + HD]
        full = jnp.concatenate([front * cos - back * sin, back * cos + front * sin], axis=0)
        return full.astype(bf16).astype(f32)

    def turned(values, offset, width):
        pieces = [values]
        if offset:
            pieces.insert(0, jnp.zeros((offset, 2 * NEW), f32))
        pieces.append(jnp.zeros((width - offset - HD, 2 * NEW), f32))
        return jnp.transpose(jnp.concatenate(pieces, axis=0)).astype(bf16)

    for g in range(G):
        q = rotated(g * HD)
        for m, (_, width, offset) in enumerate(KEY_TILE):
            qt = turned(q, offset, width)
            for a in range(2):
                qs[m, a, g * NEW : (g + 1) * NEW, :width] = qt[a * NEW : (a + 1) * NEW]
    kn[...] = turned(rotated(G * HD), 0, 128)
    vn[...] = turned(proj[(G + 1) * HD :].astype(bf16).astype(f32), 0, 128)

    t_col = iota((G * NEW, 1), 0) % NEW

    def attend(a, keys, pos_of, top0, with_window):
        length = lens_s[2 * me + a]
        cols = iota((1, 512), 1)
        top = top0
        for m, (first, width, _) in enumerate(KEY_TILE):
            s = mm(qs[m, a, :, :width], keys[:, first : first + width], ((1,), (1,)))
            rel = pos_of(cols) + m - length
            ok = rel < 0
            if with_window:
                ok = ok & (rel > t_col - WINDOW)
            s = jnp.where(ok, s, MASKED)
            sc[m] = s
            top = jnp.maximum(top, jnp.max(s, axis=1, keepdims=True))
        total = jnp.zeros((G * NEW, 1), f32)
        sums = jnp.zeros((G * NEW, 128), f32)
        for m, (first, width, offset) in enumerate(VAL_TILE):
            p = jnp.exp2((sc[m] - top) * SCALE)
            total = total + jnp.sum(p, axis=1, keepdims=True)
            o = mm(p.astype(bf16), keys[:, first : first + width], ((1,), (0,)))
            sums = sums + pltpu.roll(o, width - offset, 1)[:, :128]
        return top, total, sums

    def home(a, carry):
        at = pl.ds(pl.multiple_of(a * NEW, NEW), NEW)
        s = mm(qs[0, a, :, :128], kn[at, :], ((1,), (1,)))
        s = jnp.where(iota((G * NEW, NEW), 1) <= t_col, s, MASKED)
        top_new = jnp.max(s, axis=1, keepdims=True)
        top, total, sums = attend(
            a, xh.at[a], lambda col: (col % KEEP) * PAGE + (col // KEEP) * 4, top_new, True
        )
        p = jnp.exp2((s - top) * SCALE)
        stat[a, 0] = jnp.broadcast_to(top, (G * NEW, 128))
        stat[a, 1] = jnp.broadcast_to(total + jnp.sum(p, axis=1, keepdims=True), (G * NEW, 128))
        acc[a] = sums + mm(p.astype(bf16), vn[at, :], ((1,), (0,)))
        return carry

    lax.fori_loop(0, 2, home, 0)

    idx_copy.wait()
    for copy in copies:
        copy.wait_recv()

    def tail(a, carry):
        for j in range(TAIL):
            where = jnp.clip(idx[0, a * TAIL + j], 0, 2 * GROUPS - 1)
            xt[j * ROWS : (j + 1) * ROWS, :] = recv[where // 2, where % 2]
        old_top = stat[a, 0][:, :1]
        top, total, sums = attend(a, xt, lambda col: KEEP * PAGE + col * 4, old_top, False)
        weight = jnp.exp2((old_top - top) * SCALE)
        result = (acc[a] * weight + sums) / (stat[a, 1][:, :1] * weight + total)
        for g in range(G):
            hs[g, pl.ds(pl.multiple_of(a * NEW, NEW), NEW), :] = result[g * NEW : (g + 1) * NEW]
        return carry

    lax.fori_loop(0, 2, tail, 0)
    for g in range(G):
        ht[g * HD : (g + 1) * HD, :] = jnp.transpose(hs[g])[:HD].astype(bf16)

    def project(dest):
        rows = pl.ds(pl.multiple_of(dest * XB, 64), XB)
        return mm(wot[rows, :], ht[...], ((1,), (0,)))

    sums = []
    for k in Z_STEPS:
        dest = lax.rem(z + k, TP)
        rsend[k] = project(dest).astype(bf16)
        copy = pltpu.make_async_remote_copy(
            src_ref=rsend.at[k], dst_ref=rrecv.at[k], send_sem=rs_ss.at[k], recv_sem=rs_rs.at[k],
            device_id={"tp": dest}, device_id_type=MESH,
        )
        copy.start()
        sums.append(copy)
    total = project(z)
    for k, copy in reversed(list(zip(Z_STEPS, sums))):
        copy.wait_recv()
        total = total + rrecv[k].astype(f32)
    out_ref[...] = total

    for copy in ags + copies + sums:
        copy.wait_send()


def layer(rounds, *operands):
    any_space = pl.BlockSpec(memory_space=pl.ANY)
    vmem = pl.BlockSpec(memory_space=pltpu.VMEM)
    smem = pl.BlockSpec(memory_space=pltpu.SMEM)
    f32, bf16 = jnp.float32, jnp.bfloat16
    dma = pltpu.SemaphoreType.DMA
    return pl.pallas_call(
        functools.partial(kernel, rounds),
        out_shape=(jax.ShapeDtypeStruct((XB, 128), f32), jax.ShapeDtypeStruct((1,), jnp.int32)),
        in_specs=[any_space, vmem, any_space, any_space, any_space, vmem, vmem, vmem, smem],
        out_specs=(vmem, smem),
        scratch_shapes=[
            pltpu.VMEM((D, 128), bf16),
            pltpu.VMEM((POOL, ROWS * WIDTH), bf16),
            pltpu.VMEM((480, D), bf16),
            pltpu.VMEM((D, 128), f32),
            pltpu.VMEM((XB, D), bf16),
            pltpu.VMEM((D, XB), bf16),
            pltpu.VMEM((5, ROWS * 64, 128), f32),
            pltpu.VMEM((GROUPS, 2, ROWS, WIDTH), bf16),
            pltpu.VMEM((GROUPS, 2, ROWS, WIDTH), bf16),
            pltpu.VMEM((2, 512, WIDTH), bf16),
            pltpu.VMEM((512, WIDTH), bf16),
            pltpu.VMEM((4, 2, G * NEW, 256), bf16),
            pltpu.VMEM((128, 128), bf16),
            pltpu.VMEM((128, 128), bf16),
            pltpu.VMEM((4, G * NEW, 512), f32),
            pltpu.VMEM((2, 2, G * NEW, 128), f32),
            pltpu.VMEM((2, G * NEW, 128), f32),
            pltpu.VMEM((G, 128, 128), f32),
            pltpu.VMEM((XB, 128), bf16),
            pltpu.VMEM((TP, XB, 128), bf16),
            pltpu.VMEM((TP, XB, 128), bf16),
            pltpu.VMEM((8, 128), jnp.int32),
            pltpu.SMEM((8, 128), jnp.int32),
            dma((5,)), dma((2, 31)), dma((2, 31)), dma((TP,)), dma((TP,)), dma((TP,)), dma((TP,)),
        ],
        compiler_params=pltpu.CompilerParams(
            collective_id=rounds, has_side_effects=True, vmem_limit_bytes=60 * 2**20
        ),
        name=f"paged_prefill_{rounds}",
    )(*operands)


def local(activations, norm_gain, input_proj, output_proj, cache_pool, page_table, rebalance_plan, cached_lengths, token_positions):
    operands = (
        activations.T,
        norm_gain.reshape(20, 128),
        jnp.transpose(input_proj, (1, 2, 0)).reshape(480, D),
        output_proj,
        cache_pool.reshape(POOL, ROWS * WIDTH),
        page_table.T,
        rebalance_plan.T,
        cached_lengths.reshape(1, 64),
        cached_lengths,
    )
    out, more = layer(1, *operands)
    out = lax.cond(more[0] > 0, lambda first, *rest: layer(2, *rest)[0], lambda first, *rest: first, out, *operands)
    return out.T


def solution(mesh):
    in_specs = (
        P("req", "tp"), P(), P(None, "tp", None), P("tp", None), P("req", "tp", None), P(), P(), P(), P(),
    )
    return jax.shard_map(local, mesh=mesh, in_specs=in_specs, out_specs=P("req", "tp"), check_vma=False)
```

```python
import functools

import jax
import jax.numpy as jnp
from jax import lax
from jax.experimental import pallas as pl
from jax.experimental.pallas import tpu as pltpu
from jax.sharding import PartitionSpec as P

MESH = pl.DeviceIdType.MESH
HD = 80
HALF = 40
WINDOW = 4096
PAGE = 128
KEEP = 16
TAIL = 16
NEW = 64
G = 4
GROUPS = 32
TP = 8
POOL = 94
D = 2560
ROWS = 32
WIDTH = 640
XB = 320
EPSILON = 1e-05
LOG_THETA = 9.210340371976184
MASKED = -1e30
SCALE = HD ** (-0.5) * 1.4426950408889634
STEP = 96
KEY_TILE = ((0, 128, 0, 0), (128, 128, 128, 160), (256, 256, 256, 320), (384, 256, 512, 608))
QUERY_LANES = 768
VAL_TILE = ((0, 256, 80), (128, 256, 112), (384, 128, 16), (512, 128, 48))
OFFSETS = [(x, y, c) for x in range(4) for y in range(4) for c in range(2) if (x, y, c) != (0, 0, 0)]
OFFSETS.sort(key=lambda o: -min(o[0], 4 - o[0]) - min(o[1], 4 - o[1]))
Z_STEPS = (4, 3, 5, 2, 6, 1, 7)
STATED = (2, 0, 0)


def mm(a, b, contract):
    return lax.dot_general(a, b, (contract, ((), ())), preferred_element_type=jnp.float32)


def iota(shape, dim):
    return lax.broadcasted_iota(jnp.int32, shape, dim)


def kernel(
    rounds,
    x_hbm, gain_ref, w_hbm, wo_hbm, pool_hbm, table_ref, plan_ref, lens_ref, lens_s,
    out_ref, more_ref,
    cos_sin, xf, pool, w, gb, wo, wot, pf, send, recv, xh, xt, qs, kn, vn, sc, stat, acc, hs, ht, part, rrecv, idx_v, idx,
    load_sem, page_ss, page_rs, ag_ss, ag_rs, rs_ss, rs_rs,
):
    me = lax.axis_index("req")
    z = lax.axis_index("tp")
    mx, my, mc = me // 8, (me // 2) % 4, me % 2
    f32, bf16 = jnp.float32, jnp.bfloat16

    def peer(o):
        return ((mx + o[0]) % 4) * 8 + ((my + o[1]) % 4) * 2 + (mc + o[2]) % 2

    own = pl.ds(pl.multiple_of(z * XB, 64), XB)
    loads = [
        pltpu.make_async_copy(x_hbm, xf.at[own], load_sem.at[0]),
        pltpu.make_async_copy(pool_hbm, pool, load_sem.at[1]),
        pltpu.make_async_copy(w_hbm, w, load_sem.at[2]),
        pltpu.make_async_copy(wo_hbm, wo, load_sem.at[3]),
    ]
    for c in loads:
        c.start()
    barrier = pltpu.get_barrier_semaphore()
    for o in OFFSETS:
        pl.semaphore_signal(barrier, inc=1, device_id={"req": peer(o)}, device_id_type=MESH)
    for k in Z_STEPS:
        pl.semaphore_signal(barrier, inc=1, device_id={"tp": lax.rem(z + k, TP)}, device_id_type=MESH)

    pl.semaphore_wait(barrier, len(OFFSETS) + len(Z_STEPS))
    loads[0].wait()

    ags = []
    for k in Z_STEPS:
        copy = pltpu.make_async_remote_copy(
            src_ref=xf.at[own], dst_ref=xf.at[own], send_sem=ag_ss.at[k], recv_sem=ag_rs.at[k],
            device_id={"tp": lax.rem(z + k, TP)}, device_id_type=MESH,
        )
        copy.start()
        ags.append(copy)

    plan = plan_ref[KEEP:, :]
    page_pos = (iota((TAIL, 64), 0) + KEEP) * PAGE
    inside = page_pos < lens_ref[...]
    held = (plan == me) & inside
    held_f = held.astype(f32)
    below = (iota((TAIL, TAIL), 0) > iota((TAIL, TAIL), 1)).astype(f32)
    rank = mm(below, held_f, ((1,), (0,)))
    ones = jnp.ones((8, TAIL), f32)
    count = mm(ones, held_f, ((1,), (0,)))
    r0, r1 = iota((64, 64), 0), iota((64, 64), 1)
    rank = rank + mm(count, ((r1 % 2 == 1) & (r0 == r1 - 1)).astype(f32), ((1,), (0,)))[0:1, :]
    slot_f = table_ref[KEEP:, :].astype(f32)
    pair = (iota((64, 128), 0) // 2 == iota((64, 128), 1)).astype(f32)
    rows = []
    for c in range(2):
        value = jnp.where(held & (rank == c), slot_f, 0.0)
        rows.append(mm(mm(ones, value, ((1,), (0,))), pair, ((1,), (0,)))[0:1, :])

    lane = iota((TAIL, 64), 1)

    def own_column(values):
        cols = [jnp.sum(jnp.where(lane == 2 * me + a, values, 0.0), axis=1, keepdims=True) for a in range(2)]
        return jnp.concatenate(cols, axis=0)

    e0, e1 = iota((2 * TAIL, 128), 0), iota((2 * TAIL, 128), 1)

    def as_row(col):
        return jnp.sum(jnp.where(e0 == e1, col, 0.0), axis=0, keepdims=True)

    group_col, ok_col = own_column(plan.astype(f32)), own_column(inside.astype(f32))
    group_row = as_row(group_col)
    earlier = jnp.where((group_col == group_row) & (e0 < e1), ok_col, 0.0)
    rows.append(as_row(own_column(table_ref[:KEEP, :].astype(f32))))
    rows.append(group_row * 2.0 + as_row(ok_col) * jnp.sum(earlier, axis=0, keepdims=True))
    at_row = iota((8, 128), 0)
    lists = jnp.zeros((8, 128), f32)
    for n, row in enumerate(rows):
        lists = jnp.where(at_row == n, row, lists)
    idx_v[...] = lists.astype(jnp.int32)
    idx_copy = pltpu.make_async_copy(idx_v, idx, load_sem.at[4])
    idx_copy.start()

    loads[1].wait()

    def turn(i, carry):
        for k in range(5):
            lanes = pl.ds(pl.multiple_of(i * WIDTH + k * 128, 128), 128)
            pf[k, pl.ds(pl.multiple_of(i * STEP, 8), POOL), :] = pool[:, lanes].astype(f32)
        return carry

    lax.fori_loop(0, ROWS, turn, 0)
    idx_copy.wait()

    def page_tile(slot, k):
        return pf[k, pl.ds(jnp.clip(slot, 0, POOL - 1), ROWS, stride=STEP), :].astype(bf16)

    def slots(o):
        return 2 if rounds == 2 or o == STATED else 1

    copies = []
    for n, o in enumerate(OFFSETS):
        p = peer(o)
        for c in range(slots(o)):
            slot = idx[c, p]
            for k in range(5):
                send[p, c, :, k * 128 : (k + 1) * 128] = page_tile(slot, k)
        held_slots = pl.ds(0, slots(o))
        copy = pltpu.make_async_remote_copy(
            src_ref=send.at[p, held_slots], dst_ref=recv.at[me, held_slots],
            send_sem=page_ss.at[n], recv_sem=page_rs.at[n], device_id={"req": p}, device_id_type=MESH,
        )
        copy.start()
        copies.append(copy)

    def home_page(e, carry):
        slot = idx[2, e]
        for k in range(5):
            xh[e // KEEP, pl.ds(pl.multiple_of(e % KEEP * ROWS, ROWS), ROWS), k * 128 : (k + 1) * 128] = page_tile(slot, k)
        return carry

    lax.fori_loop(0, 2 * KEEP, home_page, 0)

    lens0, lens1 = lens_s[2 * me], lens_s[2 * me + 1]
    tok = iota((1, 2 * NEW), 1)
    places = jnp.where(tok < NEW, lens0 + tok, lens1 + tok - NEW).astype(f32)
    freq = jnp.exp(iota((HALF, 128), 0).astype(f32) * (-2.0 * LOG_THETA / HD))
    angle = freq * places
    cos_sin[0], cos_sin[1] = jnp.cos(angle), jnp.sin(angle)

    for i in range(20):
        gb[i * 128 : (i + 1) * 128, :] = jnp.transpose(jnp.broadcast_to(gain_ref[i : i + 1, :], (128, 128)))
    loads[3].wait()
    for i in range(20):
        wot[i * 128 : (i + 1) * 128, :] = jnp.transpose(wo[:, i * 128 : (i + 1) * 128])
    group = iota((GROUPS, 64), 0)
    owed = jnp.zeros((GROUPS, 64), f32)
    for j in range(KEEP, KEEP + TAIL):
        owed += ((plan_ref[j : j + 1, :] == group) & (lens_ref[...] > j * PAGE)).astype(f32)
    owed = mm(owed, (iota((64, GROUPS), 0) // 2 == iota((64, GROUPS), 1)).astype(f32), ((1,), (0,)))
    g0, g1 = iota((GROUPS, GROUPS), 0), iota((GROUPS, GROUPS), 1)
    owed = jnp.where(g0 == (g1 + GROUPS // 2) % GROUPS, 0.0, owed)
    more_ref[0] = (jnp.max(owed) > 1.5).astype(jnp.int32)

    loads[2].wait()
    for copy in ags:
        copy.wait_recv()

    xw = xf[...].astype(f32)
    rstd = lax.rsqrt(jnp.sum(xw * xw, axis=0, keepdims=True) * (1.0 / D) + EPSILON)
    normed = (xw * rstd * gb[...]).astype(bf16)
    proj = mm(w[...], normed, ((1,), (0,)))
    cos, sin = cos_sin[0], cos_sin[1]

    def rotated(first):
        front, back = proj[first : first + HALF], proj[first + HALF : first + HD]
        full = jnp.concatenate([front * cos - back * sin, back * cos + front * sin], axis=0)
        return full.astype(bf16)

    def turned(values):
        padded = jnp.concatenate([values.astype(f32), jnp.zeros((128 - HD, 2 * NEW), f32)], axis=0)
        return jnp.transpose(padded).astype(bf16)

    feature, at_lane = iota((HD, QUERY_LANES), 0), iota((HD, QUERY_LANES), 1)
    spread = feature == at_lane
    for _, _, _, stand in KEY_TILE[1:]:
        spread = spread | (feature == at_lane - stand)
    spread = spread.astype(f32).astype(bf16)
    for g in range(G):
        qt = mm(rotated(g * HD), spread, ((0,), (0,))).astype(bf16)
        for a in range(2):
            qs[a, g * NEW : (g + 1) * NEW, :] = qt[a * NEW : (a + 1) * NEW]
    kn[...] = turned(rotated(G * HD))
    vn[...] = turned(proj[(G + 1) * HD :].astype(bf16))

    t_col = iota((G * NEW, 1), 0) % NEW

    def attend(a, keys, first_pos, top0, with_window):
        length = lens_s[2 * me + a]
        cols = iota((1, 512), 1)
        top = top0
        for m, (first, width, at, _) in enumerate(KEY_TILE):
            s = mm(qs[a, :, at : at + width], keys[:, first : first + width], ((1,), (1,)))
            rel = cols * 4 + (first_pos + m) - length
            ok = rel < 0
            if with_window:
                ok = ok & (rel > t_col - WINDOW)
            s = jnp.where(ok, s, MASKED)
            sc[m] = s
            top = jnp.maximum(top, jnp.max(s, axis=1, keepdims=True))
        total = jnp.zeros((G * NEW, 1), f32)
        sums = jnp.zeros((G * NEW, 128), f32)
        for m, (first, width, offset) in enumerate(VAL_TILE):
            p = jnp.exp2((sc[m] - top) * SCALE)
            total = total + jnp.sum(p, axis=1, keepdims=True)
            o = mm(p.astype(bf16), keys[:, first : first + width], ((1,), (0,)))
            sums = sums + pltpu.roll(o, width - offset, 1)[:, :128]
        return top, total, sums

    def home(a, carry):
        at = pl.ds(pl.multiple_of(a * NEW, NEW), NEW)
        s = mm(qs[a, :, :128], kn[at, :], ((1,), (1,)))
        s = jnp.where(iota((G * NEW, NEW), 1) <= t_col, s, MASKED)
        top_new = jnp.max(s, axis=1, keepdims=True)
        top, total, sums = attend(a, xh.at[a], 0, top_new, True)
        p = jnp.exp2((s - top) * SCALE)
        stat[a, 0] = jnp.broadcast_to(top, (G * NEW, 128))
        stat[a, 1] = jnp.broadcast_to(total + jnp.sum(p, axis=1, keepdims=True), (G * NEW, 128))
        acc[a] = sums + mm(p.astype(bf16), vn[at, :], ((1,), (0,)))
        return carry

    lax.fori_loop(0, 2, home, 0)

    for copy in copies:
        copy.wait_recv()

    def tail(a, carry):
        for j in range(TAIL):
            where = jnp.clip(idx[3, a * TAIL + j], 0, 2 * GROUPS - 1)
            xt[j * ROWS : (j + 1) * ROWS, :] = recv[where // 2, where % 2]
        old_top = stat[a, 0][:, :1]
        top, total, sums = attend(a, xt, KEEP * PAGE, old_top, False)
        weight = jnp.exp2((old_top - top) * SCALE)
        result = (acc[a] * weight + sums) / (stat[a, 1][:, :1] * weight + total)
        for g in range(G):
            hs[g, pl.ds(pl.multiple_of(a * NEW, NEW), NEW), :] = result[g * NEW : (g + 1) * NEW]
        return carry

    lax.fori_loop(0, 2, tail, 0)
    for g in range(G):
        ht[g * HD : (g + 1) * HD, :] = jnp.transpose(hs[g])[:HD].astype(bf16)

    def project(dest):
        rows = pl.ds(pl.multiple_of(dest * XB, 64), XB)
        return mm(wot[rows, :], ht[...], ((1,), (0,)))

    for k in Z_STEPS:
        part[k] = project(lax.rem(z + k, TP)).astype(bf16)
    sums = []
    for k in Z_STEPS:
        copy = pltpu.make_async_remote_copy(
            src_ref=part.at[k], dst_ref=rrecv.at[k], send_sem=rs_ss.at[k], recv_sem=rs_rs.at[k],
            device_id={"tp": lax.rem(z + k, TP)}, device_id_type=MESH,
        )
        copy.start()
        sums.append(copy)
    total = project(z)
    for k, copy in reversed(list(zip(Z_STEPS, sums))):
        copy.wait_recv()
        total = total + rrecv[k].astype(f32)
    out_ref[...] = total

    for copy in ags + copies + sums:
        copy.wait_send()


def layer(rounds, *operands):
    any_space = pl.BlockSpec(memory_space=pl.ANY)
    vmem = pl.BlockSpec(memory_space=pltpu.VMEM)
    smem = pl.BlockSpec(memory_space=pltpu.SMEM)
    f32, bf16 = jnp.float32, jnp.bfloat16
    dma = pltpu.SemaphoreType.DMA
    return pl.pallas_call(
        functools.partial(kernel, rounds),
        out_shape=(jax.ShapeDtypeStruct((XB, 128), f32), jax.ShapeDtypeStruct((1,), jnp.int32)),
        in_specs=[any_space, vmem, any_space, any_space, any_space, vmem, vmem, vmem, smem],
        out_specs=(vmem, smem),
        scratch_shapes=[
            pltpu.VMEM((2, HALF, 128), f32),
            pltpu.VMEM((D, 128), bf16),
            pltpu.VMEM((POOL, ROWS * WIDTH), bf16),
            pltpu.VMEM((480, D), bf16),
            pltpu.VMEM((D, 128), f32),
            pltpu.VMEM((XB, D), bf16),
            pltpu.VMEM((D, XB), bf16),
            pltpu.VMEM((5, ROWS * STEP, 128), f32),
            pltpu.VMEM((GROUPS, 2, ROWS, WIDTH), bf16),
            pltpu.VMEM((GROUPS, 2, ROWS, WIDTH), bf16),
            pltpu.VMEM((2, 512, WIDTH), bf16),
            pltpu.VMEM((512, WIDTH), bf16),
            pltpu.VMEM((2, G * NEW, QUERY_LANES), bf16),
            pltpu.VMEM((128, 128), bf16),
            pltpu.VMEM((128, 128), bf16),
            pltpu.VMEM((4, G * NEW, 512), f32),
            pltpu.VMEM((2, 2, G * NEW, 128), f32),
            pltpu.VMEM((2, G * NEW, 128), f32),
            pltpu.VMEM((G, 128, 128), f32),
            pltpu.VMEM((XB, 128), bf16),
            pltpu.VMEM((TP, XB, 128), bf16),
            pltpu.VMEM((TP, XB, 128), bf16),
            pltpu.VMEM((8, 128), jnp.int32),
            pltpu.SMEM((8, 128), jnp.int32),
            dma((5,)), dma((31,)), dma((31,)), dma((TP,)), dma((TP,)), dma((TP,)), dma((TP,)),
        ],
        compiler_params=pltpu.CompilerParams(
            collective_id=rounds, has_side_effects=True, vmem_limit_bytes=60 * 2**20
        ),
        name=f"paged_prefill_{rounds}",
    )(*operands)


def local(activations, norm_gain, input_proj, output_proj, cache_pool, page_table, rebalance_plan, cached_lengths, token_positions):
    operands = (
        activations.T,
        norm_gain.reshape(20, 128),
        jnp.transpose(input_proj, (1, 2, 0)).reshape(480, D),
        output_proj,
        cache_pool.reshape(POOL, ROWS * WIDTH),
        page_table.T,
        rebalance_plan.T,
        cached_lengths.reshape(1, 64),
        cached_lengths,
    )
    out, more = layer(1, *operands)
    out = lax.cond(more[0] > 0, lambda first, *rest: layer(2, *rest)[0], lambda first, *rest: first, out, *operands)
    return out.T


def solution(mesh):
    in_specs = (
        P("req", "tp"), P(), P(None, "tp", None), P("tp", None), P("req", "tp", None), P(), P(), P(), P(),
    )
    return jax.shard_map(local, mesh=mesh, in_specs=in_specs, out_specs=P("req", "tp"), check_vma=False)
```

```python
import functools

import jax
import jax.numpy as jnp
from jax import lax
from jax.experimental import pallas as pl
from jax.experimental.pallas import tpu as pltpu
from jax.sharding import PartitionSpec as P

MESH = pl.DeviceIdType.MESH
HD = 80
HALF = 40
WINDOW = 4096
PAGE = 128
KEEP = 16
TAIL = 16
NEW = 64
G = 4
GROUPS = 32
TP = 8
POOL = 94
D = 2560
ROWS = 32
WIDTH = 640
XB = 320
EPSILON = 1e-05
LOG_THETA = 9.210340371976184
MASKED = -1e30
SCALE = HD ** (-0.5) * 1.4426950408889634
STEP = 97
KEY_TILE = ((0, 128, 0, 0), (128, 128, 128, 160), (256, 256, 256, 320), (384, 256, 512, 608))
QUERY_LANES = 768
VAL_TILE = ((0, 256, 80), (128, 256, 112), (384, 128, 16), (512, 128, 48))
OFFSETS = [(x, y, c) for x in range(4) for y in range(4) for c in range(2) if (x, y, c) != (0, 0, 0)]
OFFSETS.sort(key=lambda o: -min(o[0], 4 - o[0]) - min(o[1], 4 - o[1]))
PIECES = 4
STATED = (2, 0, 0)


def mm(a, b, contract):
    return lax.dot_general(a, b, (contract, ((), ())), preferred_element_type=jnp.float32)


def iota(shape, dim):
    return lax.broadcasted_iota(jnp.int32, shape, dim)


def kernel(
    rounds,
    x_hbm, gain_ref, w_hbm, wo_hbm, pool_hbm, table_ref, plan_ref, lens_ref, lens_s,
    out_ref, more_ref,
    cos_sin, xf, pool, w, gb, wo, wot, pf, send, recv, xh, xt, qs, kn, vn, sc, stat, acc, hs, ht, part, rrecv, idx_v, idx,
    load_sem, page_ss, page_rs, ag_ss, ag_rs, rs_ss, rs_rs,
):
    me = lax.axis_index("req")
    z = lax.axis_index("tp")
    mx, my, mc = me // 8, (me // 2) % 4, me % 2
    f32, bf16 = jnp.float32, jnp.bfloat16

    def peer(o):
        return ((mx + o[0]) % 4) * 8 + ((my + o[1]) % 4) * 2 + (mc + o[2]) % 2

    own = pl.ds(pl.multiple_of(z * XB, 64), XB)
    loads = [
        pltpu.make_async_copy(x_hbm, xf.at[own], load_sem.at[0]),
        pltpu.make_async_copy(pool_hbm, pool, load_sem.at[1]),
        pltpu.make_async_copy(w_hbm, w, load_sem.at[2]),
        pltpu.make_async_copy(wo_hbm, wo, load_sem.at[3]),
    ]
    for c in loads:
        c.start()
    barrier = pltpu.get_barrier_semaphore()
    for o in OFFSETS:
        pl.semaphore_signal(barrier, inc=1, device_id={"req": peer(o)}, device_id_type=MESH)
    ring = (lax.rem(z + 1, TP), lax.rem(z + TP - 1, TP))
    for n in ring:
        pl.semaphore_signal(barrier, inc=1, device_id={"tp": n}, device_id_type=MESH)

    pl.semaphore_wait(barrier, len(OFFSETS) + len(ring))
    loads[0].wait()

    ags = {}

    def ag_step(step):
        for piece in range(PIECES):
            for way in range(2):
                if step:
                    ags[step - 1, way, piece].wait_recv()
                if step < 4 - way:
                    block = lax.rem(z - step + TP, TP) if way == 0 else lax.rem(z + step, TP)
                    size = XB // PIECES
                    at = pl.ds(pl.multiple_of(block * XB + piece * size, 16), size)
                    n = (step * 2 + way) * PIECES + piece
                    copy = pltpu.make_async_remote_copy(
                        src_ref=xf.at[at], dst_ref=xf.at[at], send_sem=ag_ss.at[n], recv_sem=ag_rs.at[n],
                        device_id={"tp": ring[way]}, device_id_type=MESH,
                    )
                    copy.start()
                    ags[step, way, piece] = copy

    ag_step(0)

    plan = plan_ref[KEEP:, :]
    page_pos = (iota((TAIL, 64), 0) + KEEP) * PAGE
    inside = page_pos < lens_ref[...]
    held = (plan == me) & inside
    held_f = held.astype(f32)
    below = (iota((TAIL, TAIL), 0) > iota((TAIL, TAIL), 1)).astype(f32)
    rank = mm(below, held_f, ((1,), (0,)))
    ones = jnp.ones((8, TAIL), f32)
    count = mm(ones, held_f, ((1,), (0,)))
    r0, r1 = iota((64, 64), 0), iota((64, 64), 1)
    rank = rank + mm(count, ((r1 % 2 == 1) & (r0 == r1 - 1)).astype(f32), ((1,), (0,)))[0:1, :]
    slot_f = table_ref[KEEP:, :].astype(f32)
    pair = (iota((64, 128), 0) // 2 == iota((64, 128), 1)).astype(f32)
    rows = []
    for c in range(2):
        value = jnp.where(held & (rank == c), slot_f, 0.0)
        rows.append(mm(mm(ones, value, ((1,), (0,))), pair, ((1,), (0,)))[0:1, :])

    lane = iota((TAIL, 64), 1)

    def own_column(values):
        cols = [jnp.sum(jnp.where(lane == 2 * me + a, values, 0.0), axis=1, keepdims=True) for a in range(2)]
        return jnp.concatenate(cols, axis=0)

    e0, e1 = iota((2 * TAIL, 128), 0), iota((2 * TAIL, 128), 1)

    def as_row(col):
        return jnp.sum(jnp.where(e0 == e1, col, 0.0), axis=0, keepdims=True)

    group_col, ok_col = own_column(plan.astype(f32)), own_column(inside.astype(f32))
    group_row = as_row(group_col)
    earlier = jnp.where((group_col == group_row) & (e0 < e1), ok_col, 0.0)
    rows.append(as_row(own_column(table_ref[:KEEP, :].astype(f32))))
    rows.append(group_row * 2.0 + as_row(ok_col) * jnp.sum(earlier, axis=0, keepdims=True))
    at_row = iota((8, 128), 0)
    lists = jnp.zeros((8, 128), f32)
    for n, row in enumerate(rows):
        lists = jnp.where(at_row == n, row, lists)
    idx_v[...] = lists.astype(jnp.int32)
    idx_copy = pltpu.make_async_copy(idx_v, idx, load_sem.at[4])
    idx_copy.start()

    loads[1].wait()

    def turn(i, carry):
        for k in range(5):
            lanes = pl.ds(pl.multiple_of(i * WIDTH + k * 128, 128), 128)
            pf[k, pl.ds(i * STEP, POOL), :] = pool[:, lanes].astype(f32)
        return carry

    lax.fori_loop(0, ROWS, turn, 0)
    idx_copy.wait()

    def page_tile(slot, k):
        return pf[k, pl.ds(jnp.clip(slot, 0, POOL - 1), ROWS, stride=STEP), :].astype(bf16)

    def slots(o):
        return 2 if rounds == 2 or o == STATED else 1

    copies = []
    for n, o in enumerate(OFFSETS):
        p = peer(o)
        for c in range(slots(o)):
            slot = idx[c, p]
            for k in range(5):
                send[p, c, :, k * 128 : (k + 1) * 128] = page_tile(slot, k)
        held_slots = pl.ds(0, slots(o))
        copy = pltpu.make_async_remote_copy(
            src_ref=send.at[p, held_slots], dst_ref=recv.at[me, held_slots],
            send_sem=page_ss.at[n], recv_sem=page_rs.at[n], device_id={"req": p}, device_id_type=MESH,
        )
        copy.start()
        copies.append(copy)

    ag_step(1)

    def home_page(e, carry):
        slot = idx[2, e]
        for k in range(5):
            xh[e // KEEP, pl.ds(pl.multiple_of(e % KEEP * ROWS, ROWS), ROWS), k * 128 : (k + 1) * 128] = page_tile(slot, k)
        return carry

    lax.fori_loop(0, 2 * KEEP, home_page, 0)
    ag_step(2)

    lens0, lens1 = lens_s[2 * me], lens_s[2 * me + 1]
    tok = iota((1, 2 * NEW), 1)
    places = jnp.where(tok < NEW, lens0 + tok, lens1 + tok - NEW).astype(f32)
    freq = jnp.exp(iota((HALF, 128), 0).astype(f32) * (-2.0 * LOG_THETA / HD))
    angle = freq * places
    cos_sin[0], cos_sin[1] = jnp.cos(angle), jnp.sin(angle)

    for i in range(20):
        gb[i * 128 : (i + 1) * 128, :] = jnp.transpose(jnp.broadcast_to(gain_ref[i : i + 1, :], (128, 128)))
    ag_step(3)
    loads[3].wait()
    for i in range(20):
        wot[i * 128 : (i + 1) * 128, :] = jnp.transpose(wo[:, i * 128 : (i + 1) * 128])
    group = iota((GROUPS, 64), 0)
    owed = jnp.zeros((GROUPS, 64), f32)
    for j in range(KEEP, KEEP + TAIL):
        owed += ((plan_ref[j : j + 1, :] == group) & (lens_ref[...] > j * PAGE)).astype(f32)
    owed = mm(owed, (iota((64, GROUPS), 0) // 2 == iota((64, GROUPS), 1)).astype(f32), ((1,), (0,)))
    g0, g1 = iota((GROUPS, GROUPS), 0), iota((GROUPS, GROUPS), 1)
    owed = jnp.where(g0 == (g1 + GROUPS // 2) % GROUPS, 0.0, owed)
    more_ref[0] = (jnp.max(owed) > 1.5).astype(jnp.int32)

    loads[2].wait()
    for piece in range(PIECES):
        ags[3, 0, piece].wait_recv()

    xw = xf[...].astype(f32)
    rstd = lax.rsqrt(jnp.sum(xw * xw, axis=0, keepdims=True) * (1.0 / D) + EPSILON)
    normed = (xw * rstd * gb[...]).astype(bf16)
    proj = mm(w[...], normed, ((1,), (0,)))
    cos, sin = cos_sin[0], cos_sin[1]

    def rotated(first):
        front, back = proj[first : first + HALF], proj[first + HALF : first + HD]
        full = jnp.concatenate([front * cos - back * sin, back * cos + front * sin], axis=0)
        return full.astype(bf16)

    def turned(values):
        padded = jnp.concatenate([values.astype(f32), jnp.zeros((128 - HD, 2 * NEW), f32)], axis=0)
        return jnp.transpose(padded).astype(bf16)

    feature, at_lane = iota((HD, QUERY_LANES), 0), iota((HD, QUERY_LANES), 1)
    spread = feature == at_lane
    for _, _, _, stand in KEY_TILE[1:]:
        spread = spread | (feature == at_lane - stand)
    spread = spread.astype(f32).astype(bf16)
    for g in range(G):
        qt = mm(rotated(g * HD), spread, ((0,), (0,))).astype(bf16)
        for a in range(2):
            qs[a, g * NEW : (g + 1) * NEW, :] = qt[a * NEW : (a + 1) * NEW]
    kn[...] = turned(rotated(G * HD))
    vn[...] = turned(proj[(G + 1) * HD :].astype(bf16))

    t_col = iota((G * NEW, 1), 0) % NEW

    def attend(a, keys, first_pos, top0, with_window):
        length = lens_s[2 * me + a]
        cols = iota((1, 512), 1)
        top = top0
        for m, (first, width, at, _) in enumerate(KEY_TILE):
            s = mm(qs[a, :, at : at + width], keys[:, first : first + width], ((1,), (1,)))
            rel = cols * 4 + (first_pos + m) - length
            ok = rel < 0
            if with_window:
                ok = ok & (rel > t_col - WINDOW)
            s = jnp.where(ok, s, MASKED)
            sc[m] = s
            top = jnp.maximum(top, jnp.max(s, axis=1, keepdims=True))
        total = jnp.zeros((G * NEW, 1), f32)
        sums = jnp.zeros((G * NEW, 128), f32)
        for m, (first, width, offset) in enumerate(VAL_TILE):
            p = jnp.exp2((sc[m] - top) * SCALE)
            total = total + jnp.sum(p, axis=1, keepdims=True)
            o = mm(p.astype(bf16), keys[:, first : first + width], ((1,), (0,)))
            sums = sums + pltpu.roll(o, width - offset, 1)[:, :128]
        return top, total, sums

    def home(a, carry):
        at = pl.ds(pl.multiple_of(a * NEW, NEW), NEW)
        s = mm(qs[a, :, :128], kn[at, :], ((1,), (1,)))
        s = jnp.where(iota((G * NEW, NEW), 1) <= t_col, s, MASKED)
        top_new = jnp.max(s, axis=1, keepdims=True)
        top, total, sums = attend(a, xh.at[a], 0, top_new, True)
        p = jnp.exp2((s - top) * SCALE)
        stat[a, 0] = jnp.broadcast_to(top, (G * NEW, 128))
        stat[a, 1] = jnp.broadcast_to(total + jnp.sum(p, axis=1, keepdims=True), (G * NEW, 128))
        acc[a] = sums + mm(p.astype(bf16), vn[at, :], ((1,), (0,)))
        return carry

    lax.fori_loop(0, 2, home, 0)

    for copy in copies:
        copy.wait_recv()

    def tail(a, carry):
        for j in range(TAIL):
            where = jnp.clip(idx[3, a * TAIL + j], 0, 2 * GROUPS - 1)
            xt[j * ROWS : (j + 1) * ROWS, :] = recv[where // 2, where % 2]
        old_top = stat[a, 0][:, :1]
        top, total, sums = attend(a, xt, KEEP * PAGE, old_top, False)
        weight = jnp.exp2((old_top - top) * SCALE)
        result = (acc[a] * weight + sums) / (stat[a, 1][:, :1] * weight + total)
        for g in range(G):
            hs[g, pl.ds(pl.multiple_of(a * NEW, NEW), NEW), :] = result[g * NEW : (g + 1) * NEW]
        return carry

    lax.fori_loop(0, 2, tail, 0)
    for g in range(G):
        ht[g * HD : (g + 1) * HD, :] = jnp.transpose(hs[g])[:HD].astype(bf16)

    def project(dest):
        rows = pl.ds(pl.multiple_of(dest * XB, 64), XB)
        return mm(wot[rows, :], ht[...], ((1,), (0,)))

    size = XB // PIECES
    sums = {}
    for step in range(4):
        for way in range(2):
            hop = step - way
            if hop < 0:
                continue
            mine = project(lax.rem(z + 4 - hop, TP) if way == 0 else lax.rem(z + TP - 3 + hop, TP))
            for piece in range(PIECES):
                n = (hop * 2 + way) * PIECES + piece
                block = mine[piece * size : (piece + 1) * size]
                if hop:
                    sums[hop - 1, way, piece].wait_recv()
                    block = block + rrecv[n - 2 * PIECES].astype(f32)
                part[n] = block.astype(bf16)
                copy = pltpu.make_async_remote_copy(
                    src_ref=part.at[n], dst_ref=rrecv.at[n], send_sem=rs_ss.at[n], recv_sem=rs_rs.at[n],
                    device_id={"tp": ring[way]}, device_id_type=MESH,
                )
                copy.start()
                sums[hop, way, piece] = copy
    mine = project(z)
    for piece in range(PIECES):
        block = mine[piece * size : (piece + 1) * size]
        for hop, way in ((2, 1), (3, 0)):
            sums[hop, way, piece].wait_recv()
            block = block + rrecv[(hop * 2 + way) * PIECES + piece].astype(f32)
        out_ref[piece * size : (piece + 1) * size, :] = block

    for copy in list(ags.values()) + copies + list(sums.values()):
        copy.wait_send()


def layer(rounds, *operands):
    any_space = pl.BlockSpec(memory_space=pl.ANY)
    vmem = pl.BlockSpec(memory_space=pltpu.VMEM)
    smem = pl.BlockSpec(memory_space=pltpu.SMEM)
    f32, bf16 = jnp.float32, jnp.bfloat16
    dma = pltpu.SemaphoreType.DMA
    return pl.pallas_call(
        functools.partial(kernel, rounds),
        out_shape=(jax.ShapeDtypeStruct((XB, 128), f32), jax.ShapeDtypeStruct((1,), jnp.int32)),
        in_specs=[any_space, vmem, any_space, any_space, any_space, vmem, vmem, vmem, smem],
        out_specs=(vmem, smem),
        scratch_shapes=[
            pltpu.VMEM((2, HALF, 128), f32),
            pltpu.VMEM((D, 128), bf16),
            pltpu.VMEM((POOL, ROWS * WIDTH), bf16),
            pltpu.VMEM((480, D), bf16),
            pltpu.VMEM((D, 128), f32),
            pltpu.VMEM((XB, D), bf16),
            pltpu.VMEM((D, XB), bf16),
            pltpu.VMEM((5, ROWS * STEP + 8, 128), f32),
            pltpu.VMEM((GROUPS, 2, ROWS, WIDTH), bf16),
            pltpu.VMEM((GROUPS, 2, ROWS, WIDTH), bf16),
            pltpu.VMEM((2, 512, WIDTH), bf16),
            pltpu.VMEM((512, WIDTH), bf16),
            pltpu.VMEM((2, G * NEW, QUERY_LANES), bf16),
            pltpu.VMEM((128, 128), bf16),
            pltpu.VMEM((128, 128), bf16),
            pltpu.VMEM((4, G * NEW, 512), f32),
            pltpu.VMEM((2, 2, G * NEW, 128), f32),
            pltpu.VMEM((2, G * NEW, 128), f32),
            pltpu.VMEM((G, 128, 128), f32),
            pltpu.VMEM((XB, 128), bf16),
            pltpu.VMEM((8 * PIECES, XB // PIECES, 128), bf16),
            pltpu.VMEM((8 * PIECES, XB // PIECES, 128), bf16),
            pltpu.VMEM((8, 128), jnp.int32),
            pltpu.SMEM((8, 128), jnp.int32),
            dma((5,)), dma((31,)), dma((31,)), *[dma((8 * PIECES,))] * 4,
        ],
        compiler_params=pltpu.CompilerParams(
            collective_id=rounds, has_side_effects=True, vmem_limit_bytes=60 * 2**20
        ),
        name=f"paged_prefill_{rounds}",
    )(*operands)


def local(activations, norm_gain, input_proj, output_proj, cache_pool, page_table, rebalance_plan, cached_lengths, token_positions):
    operands = (
        activations.T,
        norm_gain.reshape(20, 128),
        jnp.transpose(input_proj, (1, 2, 0)).reshape(480, D),
        output_proj,
        cache_pool.reshape(POOL, ROWS * WIDTH),
        page_table.T,
        rebalance_plan.T,
        cached_lengths.reshape(1, 64),
        cached_lengths,
    )
    out, more = layer(1, *operands)
    out = lax.cond(more[0] > 0, lambda first, *rest: layer(2, *rest)[0], lambda first, *rest: first, out, *operands)
    return out.T


def solution(mesh):
    in_specs = (
        P("req", "tp"), P(), P(None, "tp", None), P("tp", None), P("req", "tp", None), P(), P(), P(), P(),
    )
    return jax.shard_map(local, mesh=mesh, in_specs=in_specs, out_specs=P("req", "tp"), check_vma=False)
```

```python
import functools

import jax
import jax.numpy as jnp
from jax import lax
from jax.experimental import pallas as pl
from jax.experimental.pallas import tpu as pltpu
from jax.sharding import PartitionSpec as P

MESH = pl.DeviceIdType.MESH
HD = 80
HALF = 40
WINDOW = 4096
PAGE = 128
KEEP = 16
TAIL = 16
NEW = 64
G = 4
GROUPS = 32
TP = 8
POOL = 94
D = 2560
ROWS = 32
WIDTH = 640
XB = 320
EPSILON = 1e-05
LOG_THETA = 9.210340371976184
MASKED = -1e30
SCALE = HD ** (-0.5) * 1.4426950408889634
STEP = 97
KEY_TILE = ((0, 128, 0, 0), (128, 128, 128, 160), (256, 256, 256, 320), (384, 256, 512, 608))
QUERY_LANES = 768
VAL_TILE = ((0, 256, 80), (128, 256, 112), (384, 128, 16), (512, 128, 48))
OFFSETS = [(x, y, c) for x in range(4) for y in range(4) for c in range(2) if (x, y, c) != (0, 0, 0)]
OFFSETS.sort(key=lambda o: -min(o[0], 4 - o[0]) - min(o[1], 4 - o[1]))
PIECES = 2
STATED = (2, 0, 0)


def mm(a, b, contract):
    return lax.dot_general(a, b, (contract, ((), ())), preferred_element_type=jnp.float32)


def iota(shape, dim):
    return lax.broadcasted_iota(jnp.int32, shape, dim)


def kernel(
    rounds,
    x_hbm, gain_hbm, w_hbm, wo_hbm, pool_hbm, table_hbm, plan_hbm, lens_hbm,
    out_ref, more_ref,
    gain_ref, table_ref, plan_ref, lens_ref, cos_sin, xf, pool, w, gb, wo, wot, pf, send, recv, xh, xt, qs, kn, vn, sc, stat, acc, hs, ht, mine, part, rrecv, idx_v, idx,
    load_sem, page_ss, page_rs, ag_ss, ag_rs, rs_ss, rs_rs,
):
    me = lax.axis_index("req")
    z = lax.axis_index("tp")
    mx, my, mc = me // 8, (me // 2) % 4, me % 2
    f32, bf16 = jnp.float32, jnp.bfloat16

    def peer(o):
        return ((mx + o[0]) % 4) * 8 + ((my + o[1]) % 4) * 2 + (mc + o[2]) % 2

    own = pl.ds(pl.multiple_of(z * XB, 64), XB)
    loads = [
        pltpu.make_async_copy(x_hbm, xf.at[own], load_sem.at[0]),
        pltpu.make_async_copy(pool_hbm, pool, load_sem.at[1]),
        pltpu.make_async_copy(w_hbm, w, load_sem.at[2]),
        pltpu.make_async_copy(wo_hbm, wo, load_sem.at[3]),
        pltpu.make_async_copy(table_hbm, table_ref, load_sem.at[5]),
        pltpu.make_async_copy(plan_hbm, plan_ref, load_sem.at[6]),
        pltpu.make_async_copy(lens_hbm, lens_ref, load_sem.at[7]),
        pltpu.make_async_copy(gain_hbm, gain_ref, load_sem.at[8]),
    ]
    for n in (0, 4, 5, 6, 1, 7, 2, 3):
        loads[n].start()
    barrier = pltpu.get_barrier_semaphore()
    for o in OFFSETS:
        pl.semaphore_signal(barrier, inc=1, device_id={"req": peer(o)}, device_id_type=MESH)
    ring = (lax.rem(z + 1, TP), lax.rem(z + TP - 1, TP))
    for n in ring:
        pl.semaphore_signal(barrier, inc=1, device_id={"tp": n}, device_id_type=MESH)

    pl.semaphore_wait(barrier, len(OFFSETS) + len(ring))
    loads[0].wait()

    def crosses(way, piece):
        return (piece < PIECES // 2) == (way == 0)

    ags = {}

    def ag_step(step):
        for piece in range(PIECES):
            for way in range(2):
                if step:
                    ags[step - 1, way, piece].wait_recv()
                if step < 3 or crosses(way, piece):
                    block = lax.rem(z - step + TP, TP) if way == 0 else lax.rem(z + step, TP)
                    size = XB // PIECES
                    at = pl.ds(pl.multiple_of(block * XB + piece * size, 16), size)
                    n = (step * 2 + way) * PIECES + piece
                    copy = pltpu.make_async_remote_copy(
                        src_ref=xf.at[at], dst_ref=xf.at[at], send_sem=ag_ss.at[n], recv_sem=ag_rs.at[n],
                        device_id={"tp": ring[way]}, device_id_type=MESH,
                    )
                    copy.start()
                    ags[step, way, piece] = copy

    ag_step(0)

    for n in (4, 5, 6):
        loads[n].wait()

    plan = plan_ref[KEEP:, :]
    page_pos = (iota((TAIL, 64), 0) + KEEP) * PAGE
    inside = page_pos < lens_ref[...]
    held = (plan == me) & inside
    held_f = held.astype(f32)
    below = (iota((TAIL, TAIL), 0) > iota((TAIL, TAIL), 1)).astype(f32)
    rank = mm(below, held_f, ((1,), (0,)))
    ones = jnp.ones((8, TAIL), f32)
    count = mm(ones, held_f, ((1,), (0,)))
    r0, r1 = iota((64, 64), 0), iota((64, 64), 1)
    rank = rank + mm(count, ((r1 % 2 == 1) & (r0 == r1 - 1)).astype(f32), ((1,), (0,)))[0:1, :]
    slot_f = table_ref[KEEP:, :].astype(f32)
    pair = (iota((64, 128), 0) // 2 == iota((64, 128), 1)).astype(f32)
    rows = []
    for c in range(2):
        value = jnp.where(held & (rank == c), slot_f, 0.0)
        rows.append(mm(mm(ones, value, ((1,), (0,))), pair, ((1,), (0,)))[0:1, :])

    lane = iota((TAIL, 64), 1)

    def own_column(values):
        cols = [jnp.sum(jnp.where(lane == 2 * me + a, values, 0.0), axis=1, keepdims=True) for a in range(2)]
        return jnp.concatenate(cols, axis=0)

    e0, e1 = iota((2 * TAIL, 128), 0), iota((2 * TAIL, 128), 1)

    def as_row(col):
        return jnp.sum(jnp.where(e0 == e1, col, 0.0), axis=0, keepdims=True)

    group_col, ok_col = own_column(plan.astype(f32)), own_column(inside.astype(f32))
    group_row = as_row(group_col)
    earlier = jnp.where((group_col == group_row) & (e0 < e1), ok_col, 0.0)
    rows.append(as_row(own_column(table_ref[:KEEP, :].astype(f32))))
    rows.append(group_row * 2.0 + as_row(ok_col) * jnp.sum(earlier, axis=0, keepdims=True))
    rows.append(jnp.concatenate([lens_ref[...].astype(f32), jnp.zeros((1, 64), f32)], axis=1))
    at_row = iota((8, 128), 0)
    lists = jnp.zeros((8, 128), f32)
    for n, row in enumerate(rows):
        lists = jnp.where(at_row == n, row, lists)
    idx_v[...] = lists.astype(jnp.int32)
    idx_copy = pltpu.make_async_copy(idx_v, idx, load_sem.at[4])
    idx_copy.start()

    loads[1].wait()

    def turn(i, carry):
        for k in range(5):
            lanes = pl.ds(pl.multiple_of(i * WIDTH + k * 128, 128), 128)
            pf[k, pl.ds(i * STEP, POOL), :] = pool[:, lanes].astype(f32)
        return carry

    lax.fori_loop(0, ROWS, turn, 0)
    idx_copy.wait()

    def page_tile(slot, k):
        return pf[k, pl.ds(jnp.clip(slot, 0, POOL - 1), ROWS, stride=STEP), :].astype(bf16)

    def slots(o):
        return 2 if rounds == 2 or o == STATED else 1

    copies = []
    for n, o in enumerate(OFFSETS):
        p = peer(o)
        for c in range(slots(o)):
            slot = idx[c, p]
            for k in range(5):
                send[p, c, :, k * 128 : (k + 1) * 128] = page_tile(slot, k)
        held_slots = pl.ds(0, slots(o))
        copy = pltpu.make_async_remote_copy(
            src_ref=send.at[p, held_slots], dst_ref=recv.at[me, held_slots],
            send_sem=page_ss.at[n], recv_sem=page_rs.at[n], device_id={"req": p}, device_id_type=MESH,
        )
        copy.start()
        copies.append(copy)

    ag_step(1)

    def home_page(e, carry):
        slot = idx[2, e]
        for k in range(5):
            xh[e // KEEP, pl.ds(pl.multiple_of(e % KEEP * ROWS, ROWS), ROWS), k * 128 : (k + 1) * 128] = page_tile(slot, k)
        return carry

    lax.fori_loop(0, 2 * KEEP, home_page, 0)
    ag_step(2)

    lens0, lens1 = idx[4, 2 * me], idx[4, 2 * me + 1]
    tok = iota((1, 2 * NEW), 1)
    places = jnp.where(tok < NEW, lens0 + tok, lens1 + tok - NEW).astype(f32)
    freq = jnp.exp(iota((HALF, 128), 0).astype(f32) * (-2.0 * LOG_THETA / HD))
    angle = freq * places
    cos_sin[0], cos_sin[1] = jnp.cos(angle), jnp.sin(angle)

    loads[7].wait()

    for i in range(20):
        gb[i * 128 : (i + 1) * 128, :] = jnp.transpose(jnp.broadcast_to(gain_ref[i : i + 1, :], (128, 128)))
    ag_step(3)
    loads[3].wait()
    for i in range(20):
        wot[i * 128 : (i + 1) * 128, :] = jnp.transpose(wo[:, i * 128 : (i + 1) * 128])
    group = iota((GROUPS, 64), 0)
    owed = jnp.zeros((GROUPS, 64), f32)
    for j in range(KEEP, KEEP + TAIL):
        owed += ((plan_ref[j : j + 1, :] == group) & (lens_ref[...] > j * PAGE)).astype(f32)
    owed = mm(owed, (iota((64, GROUPS), 0) // 2 == iota((64, GROUPS), 1)).astype(f32), ((1,), (0,)))
    g0, g1 = iota((GROUPS, GROUPS), 0), iota((GROUPS, GROUPS), 1)
    owed = jnp.where(g0 == (g1 + GROUPS // 2) % GROUPS, 0.0, owed)
    more_ref[0] = (jnp.max(owed) > 1.5).astype(jnp.int32)

    loads[2].wait()
    for piece in range(PIECES):
        ags[3, int(not crosses(0, piece)), piece].wait_recv()

    xw = xf[...].astype(f32)
    rstd = lax.rsqrt(jnp.sum(xw * xw, axis=0, keepdims=True) * (1.0 / D) + EPSILON)
    normed = (xw * rstd * gb[...]).astype(bf16)
    proj = mm(w[...], normed, ((1,), (0,)))
    cos, sin = cos_sin[0], cos_sin[1]

    def rotated(first):
        front, back = proj[first : first + HALF], proj[first + HALF : first + HD]
        full = jnp.concatenate([front * cos - back * sin, back * cos + front * sin], axis=0)
        return full.astype(bf16)

    def turned(values):
        padded = jnp.concatenate([values.astype(f32), jnp.zeros((128 - HD, 2 * NEW), f32)], axis=0)
        return jnp.transpose(padded).astype(bf16)

    feature, at_lane = iota((HD, QUERY_LANES), 0), iota((HD, QUERY_LANES), 1)
    spread = feature == at_lane
    for _, _, _, stand in KEY_TILE[1:]:
        spread = spread | (feature == at_lane - stand)
    spread = spread.astype(f32).astype(bf16)
    for g in range(G):
        qt = mm(rotated(g * HD), spread, ((0,), (0,))).astype(bf16)
        for a in range(2):
            qs[a, g * NEW : (g + 1) * NEW, :] = qt[a * NEW : (a + 1) * NEW]
    kn[...] = turned(rotated(G * HD))
    vn[...] = turned(proj[(G + 1) * HD :].astype(bf16))

    t_col = iota((G * NEW, 1), 0) % NEW

    def attend(a, keys, first_pos, top0, with_window):
        length = idx[4, 2 * me + a]
        cols = iota((1, 512), 1)
        top = top0
        for m, (first, width, at, _) in enumerate(KEY_TILE):
            s = mm(qs[a, :, at : at + width], keys[:, first : first + width], ((1,), (1,)))
            rel = cols * 4 + (first_pos + m) - length
            ok = rel < 0
            if with_window:
                ok = ok & (rel > t_col - WINDOW)
            s = jnp.where(ok, s, MASKED)
            sc[m] = s
            top = jnp.maximum(top, jnp.max(s, axis=1, keepdims=True))
        total = jnp.zeros((G * NEW, 1), f32)
        sums = jnp.zeros((G * NEW, 128), f32)
        for m, (first, width, offset) in enumerate(VAL_TILE):
            p = jnp.exp2((sc[m] - top) * SCALE)
            total = total + jnp.sum(p, axis=1, keepdims=True)
            o = mm(p.astype(bf16), keys[:, first : first + width], ((1,), (0,)))
            sums = sums + pltpu.roll(o, width - offset, 1)[:, :128]
        return top, total, sums

    def home(a, carry):
        at = pl.ds(pl.multiple_of(a * NEW, NEW), NEW)
        s = mm(qs[a, :, :128], kn[at, :], ((1,), (1,)))
        s = jnp.where(iota((G * NEW, NEW), 1) <= t_col, s, MASKED)
        top_new = jnp.max(s, axis=1, keepdims=True)
        top, total, sums = attend(a, xh.at[a], 0, top_new, True)
        p = jnp.exp2((s - top) * SCALE)
        stat[a, 0] = jnp.broadcast_to(top, (G * NEW, 128))
        stat[a, 1] = jnp.broadcast_to(total + jnp.sum(p, axis=1, keepdims=True), (G * NEW, 128))
        acc[a] = sums + mm(p.astype(bf16), vn[at, :], ((1,), (0,)))
        return carry

    lax.fori_loop(0, 2, home, 0)

    for copy in copies:
        copy.wait_recv()

    def tail(a, carry):
        for j in range(TAIL):
            where = jnp.clip(idx[3, a * TAIL + j], 0, 2 * GROUPS - 1)
            xt[j * ROWS : (j + 1) * ROWS, :] = recv[where // 2, where % 2]
        old_top = stat[a, 0][:, :1]
        top, total, sums = attend(a, xt, KEEP * PAGE, old_top, False)
        weight = jnp.exp2((old_top - top) * SCALE)
        result = (acc[a] * weight + sums) / (stat[a, 1][:, :1] * weight + total)
        for g in range(G):
            hs[g, pl.ds(pl.multiple_of(a * NEW, NEW), NEW), :] = result[g * NEW : (g + 1) * NEW]
        return carry

    lax.fori_loop(0, 2, tail, 0)
    for g in range(G):
        ht[g * HD : (g + 1) * HD, :] = jnp.transpose(hs[g])[:HD].astype(bf16)

    def project(k):
        rows = pl.ds(pl.multiple_of(lax.rem(z + k, TP) * XB, 64), XB)
        return mm(wot[rows, :], ht[...], ((1,), (0,)))

    size = XB // PIECES
    sums = {}
    for hop in range(4):
        if hop < 2:
            for k in ((4,), (3, 5, 2, 6, 1, 7, 0))[hop]:
                mine[k] = project(k)
        for piece in range(PIECES):
            for way in range(2):
                if hop == 0 and not crosses(way, piece):
                    continue
                n = (hop * 2 + way) * PIECES + piece
                block = mine[4 - hop if way == 0 else 4 + hop, piece * size : (piece + 1) * size, :]
                if (hop - 1, way, piece) in sums:
                    sums[hop - 1, way, piece].wait_recv()
                    block = block + rrecv[n - 2 * PIECES].astype(f32)
                part[n] = block.astype(bf16)
                copy = pltpu.make_async_remote_copy(
                    src_ref=part.at[n], dst_ref=rrecv.at[n], send_sem=rs_ss.at[n], recv_sem=rs_rs.at[n],
                    device_id={"tp": ring[way]}, device_id_type=MESH,
                )
                copy.start()
                sums[hop, way, piece] = copy
    for piece in range(PIECES):
        block = mine[0, piece * size : (piece + 1) * size, :]
        for way in range(2):
            sums[3, way, piece].wait_recv()
            block = block + rrecv[(6 + way) * PIECES + piece].astype(f32)
        out_ref[piece * size : (piece + 1) * size, :] = block

    for copy in list(ags.values()) + copies + list(sums.values()):
        copy.wait_send()


def layer(rounds, *operands):
    any_space = pl.BlockSpec(memory_space=pl.ANY)
    vmem = pl.BlockSpec(memory_space=pltpu.VMEM)
    smem = pl.BlockSpec(memory_space=pltpu.SMEM)
    f32, bf16 = jnp.float32, jnp.bfloat16
    dma = pltpu.SemaphoreType.DMA
    return pl.pallas_call(
        functools.partial(kernel, rounds),
        out_shape=(pltpu.VMEM((XB, 128), f32), jax.ShapeDtypeStruct((1,), jnp.int32)),
        in_specs=[any_space] * 8,
        out_specs=(vmem, smem),
        scratch_shapes=[
            pltpu.VMEM((20, 128), f32),
            pltpu.VMEM((32, 64), jnp.int32),
            pltpu.VMEM((32, 64), jnp.int32),
            pltpu.VMEM((1, 64), jnp.int32),
            pltpu.VMEM((2, HALF, 128), f32),
            pltpu.VMEM((D, 128), bf16),
            pltpu.VMEM((POOL, ROWS * WIDTH), bf16),
            pltpu.VMEM((480, D), bf16),
            pltpu.VMEM((D, 128), f32),
            pltpu.VMEM((XB, D), bf16),
            pltpu.VMEM((D, XB), bf16),
            pltpu.VMEM((5, ROWS * STEP + 8, 128), f32),
            pltpu.VMEM((GROUPS, 2, ROWS, WIDTH), bf16),
            pltpu.VMEM((GROUPS, 2, ROWS, WIDTH), bf16),
            pltpu.VMEM((2, 512, WIDTH), bf16),
            pltpu.VMEM((512, WIDTH), bf16),
            pltpu.VMEM((2, G * NEW, QUERY_LANES), bf16),
            pltpu.VMEM((128, 128), bf16),
            pltpu.VMEM((128, 128), bf16),
            pltpu.VMEM((4, G * NEW, 512), f32),
            pltpu.VMEM((2, 2, G * NEW, 128), f32),
            pltpu.VMEM((2, G * NEW, 128), f32),
            pltpu.VMEM((G, 128, 128), f32),
            pltpu.VMEM((XB, 128), bf16),
            pltpu.VMEM((TP, XB, 128), f32),
            pltpu.VMEM((8 * PIECES, XB // PIECES, 128), bf16),
            pltpu.VMEM((8 * PIECES, XB // PIECES, 128), bf16),
            pltpu.VMEM((8, 128), jnp.int32),
            pltpu.SMEM((8, 128), jnp.int32),
            dma((9,)), dma((31,)), dma((31,)), *[dma((8 * PIECES,))] * 4,
        ],
        compiler_params=pltpu.CompilerParams(
            collective_id=rounds, has_side_effects=True, vmem_limit_bytes=60 * 2**20
        ),
        name=f"paged_prefill_{rounds}",
    )(*operands)


def local(activations, norm_gain, input_proj, output_proj, cache_pool, page_table, rebalance_plan, cached_lengths, token_positions):
    operands = (
        activations.T,
        norm_gain.reshape(20, 128),
        jnp.transpose(input_proj, (1, 2, 0)).reshape(480, D),
        output_proj,
        cache_pool.reshape(POOL, ROWS * WIDTH),
        page_table.T,
        rebalance_plan.T,
        cached_lengths.reshape(1, 64),
    )
    out, more = layer(1, *operands)
    out = lax.cond(more[0] > 0, lambda first, *rest: layer(2, *rest)[0], lambda first, *rest: first, out, *operands)
    return out.T


def solution(mesh):
    in_specs = (
        P("req", "tp"), P(), P(None, "tp", None), P("tp", None), P("req", "tp", None), P(), P(), P(), P(),
    )
    return jax.shard_map(local, mesh=mesh, in_specs=in_specs, out_specs=P("req", "tp"), check_vma=False)
```

```python
import functools

import jax
import jax.numpy as jnp
from jax import lax
from jax.experimental import pallas as pl
from jax.experimental.pallas import tpu as pltpu
from jax.sharding import PartitionSpec as P

MESH = pl.DeviceIdType.MESH
HD = 80
HALF = 40
WINDOW = 4096
PAGE = 128
KEEP = 16
TAIL = 16
NEW = 64
G = 4
GROUPS = 32
TP = 8
POOL = 94
D = 2560
ROWS = 32
WIDTH = 640
XB = 320
EPSILON = 1e-05
LOG_THETA = 9.210340371976184
MASKED = -1e30
SCALE = HD ** (-0.5) * 1.4426950408889634
STEP = 97
KEY_TILE = ((0, 128, 0, 0), (128, 128, 128, 160), (256, 256, 256, 320), (384, 256, 512, 608))
QUERY_LANES = 768
VAL_TILE = ((0, 256, 80), (128, 256, 112), (384, 128, 16), (512, 128, 48))
OFFSETS = [(x, y, c) for x in range(4) for y in range(4) for c in range(2) if (x, y, c) != (0, 0, 0)]
OFFSETS.sort(key=lambda o: -min(o[0], 4 - o[0]) - min(o[1], 4 - o[1]))
PIECES = 2
STATED = (2, 0, 0)


def mm(a, b, contract):
    return lax.dot_general(a, b, (contract, ((), ())), preferred_element_type=jnp.float32)


def iota(shape, dim):
    return lax.broadcasted_iota(jnp.int32, shape, dim)


def kernel(
    rounds,
    x_hbm, gain_hbm, w_hbm, wo_hbm, pool_hbm, table_hbm, plan_hbm, lens_hbm,
    out_ref, more_ref,
    gain_ref, table_ref, plan_ref, lens_ref, cos_sin, xf, pool, w, gb, wo, wot, pf, send, recv, xh, xt, qs, kn, vn, sc, stat, acc, hs, ht, mine, part, rrecv, idx_v, idx,
    load_sem, page_ss, page_rs, ag_ss, ag_rs, rs_ss, rs_rs,
):
    me = lax.axis_index("req")
    z = lax.axis_index("tp")
    mx, my, mc = me // 8, (me // 2) % 4, me % 2
    f32, bf16 = jnp.float32, jnp.bfloat16

    def peer(o):
        return ((mx + o[0]) % 4) * 8 + ((my + o[1]) % 4) * 2 + (mc + o[2]) % 2

    own = pl.ds(pl.multiple_of(z * XB, 64), XB)
    halves = [pl.ds(h * ROWS // 2 * WIDTH, ROWS // 2 * WIDTH) for h in range(2)]
    loads = [
        pltpu.make_async_copy(x_hbm, xf.at[own], load_sem.at[0]),
        pltpu.make_async_copy(pool_hbm.at[:, halves[0]], pool.at[:, halves[0]], load_sem.at[1]),
        pltpu.make_async_copy(w_hbm, w, load_sem.at[2]),
        pltpu.make_async_copy(wo_hbm, wo, load_sem.at[3]),
        pltpu.make_async_copy(table_hbm, table_ref, load_sem.at[5]),
        pltpu.make_async_copy(plan_hbm, plan_ref, load_sem.at[6]),
        pltpu.make_async_copy(lens_hbm, lens_ref, load_sem.at[7]),
        pltpu.make_async_copy(gain_hbm, gain_ref, load_sem.at[8]),
        pltpu.make_async_copy(pool_hbm.at[:, halves[1]], pool.at[:, halves[1]], load_sem.at[9]),
    ]
    for n in (0, 4, 5, 6, 1, 8, 7, 2, 3):
        loads[n].start()
    barrier = pltpu.get_barrier_semaphore()
    for o in OFFSETS:
        pl.semaphore_signal(barrier, inc=1, device_id={"req": peer(o)}, device_id_type=MESH)
    ring = (lax.rem(z + 1, TP), lax.rem(z + TP - 1, TP))
    for n in ring:
        pl.semaphore_signal(barrier, inc=1, device_id={"tp": n}, device_id_type=MESH)

    pl.semaphore_wait(barrier, len(OFFSETS) + len(ring))
    loads[0].wait()

    def crosses(way, piece):
        return (piece < PIECES // 2) == (way == 0)

    ags = {}

    def ag_step(step):
        for piece in range(PIECES):
            for way in range(2):
                if step:
                    ags[step - 1, way, piece].wait_recv()
                if step < 3 or crosses(way, piece):
                    block = lax.rem(z - step + TP, TP) if way == 0 else lax.rem(z + step, TP)
                    size = XB // PIECES
                    at = pl.ds(pl.multiple_of(block * XB + piece * size, 16), size)
                    n = (step * 2 + way) * PIECES + piece
                    copy = pltpu.make_async_remote_copy(
                        src_ref=xf.at[at], dst_ref=xf.at[at], send_sem=ag_ss.at[n], recv_sem=ag_rs.at[n],
                        device_id={"tp": ring[way]}, device_id_type=MESH,
                    )
                    copy.start()
                    ags[step, way, piece] = copy

    ag_step(0)

    for n in (4, 5, 6):
        loads[n].wait()

    plan = plan_ref[KEEP:, :]
    page_pos = (iota((TAIL, 64), 0) + KEEP) * PAGE
    inside = page_pos < lens_ref[...]
    held = (plan == me) & inside
    held_f = held.astype(f32)
    below = (iota((TAIL, TAIL), 0) > iota((TAIL, TAIL), 1)).astype(f32)
    rank = mm(below, held_f, ((1,), (0,)))
    ones = jnp.ones((8, TAIL), f32)
    count = mm(ones, held_f, ((1,), (0,)))
    r0, r1 = iota((64, 64), 0), iota((64, 64), 1)
    rank = rank + mm(count, ((r1 % 2 == 1) & (r0 == r1 - 1)).astype(f32), ((1,), (0,)))[0:1, :]
    slot_f = table_ref[KEEP:, :].astype(f32)
    pair = (iota((64, 128), 0) // 2 == iota((64, 128), 1)).astype(f32)
    rows = []
    for c in range(2):
        value = jnp.where(held & (rank == c), slot_f, 0.0)
        rows.append(mm(mm(ones, value, ((1,), (0,))), pair, ((1,), (0,)))[0:1, :])

    lane = iota((TAIL, 64), 1)

    def own_column(values):
        cols = [jnp.sum(jnp.where(lane == 2 * me + a, values, 0.0), axis=1, keepdims=True) for a in range(2)]
        return jnp.concatenate(cols, axis=0)

    e0, e1 = iota((2 * TAIL, 128), 0), iota((2 * TAIL, 128), 1)

    def as_row(col):
        return jnp.sum(jnp.where(e0 == e1, col, 0.0), axis=0, keepdims=True)

    group_col, ok_col = own_column(plan.astype(f32)), own_column(inside.astype(f32))
    group_row = as_row(group_col)
    earlier = jnp.where((group_col == group_row) & (e0 < e1), ok_col, 0.0)
    rows.append(as_row(own_column(table_ref[:KEEP, :].astype(f32))))
    rows.append(group_row * 2.0 + as_row(ok_col) * jnp.sum(earlier, axis=0, keepdims=True))
    rows.append(jnp.concatenate([lens_ref[...].astype(f32), jnp.zeros((1, 64), f32)], axis=1))
    at_row = iota((8, 128), 0)
    lists = jnp.zeros((8, 128), f32)
    for n, row in enumerate(rows):
        lists = jnp.where(at_row == n, row, lists)
    idx_v[...] = lists.astype(jnp.int32)
    idx_copy = pltpu.make_async_copy(idx_v, idx, load_sem.at[4])
    idx_copy.start()

    def turn(i, carry):
        for k in range(5):
            lanes = pl.ds(pl.multiple_of(i * WIDTH + k * 128, 128), 128)
            pf[k, pl.ds(i * STEP, POOL), :] = pool[:, lanes].astype(f32)
        return carry

    def page_tile(slot, k):
        return pf[k, pl.ds(jnp.clip(slot, 0, POOL - 1), ROWS, stride=STEP), :].astype(bf16)

    def slots(o):
        return 2 if rounds == 2 or o == STATED else 1

    copies = []
    for half, load in enumerate((loads[1], loads[8])):
        load.wait()
        first, count = half * ROWS // 2, ROWS // 2
        lax.fori_loop(first, first + count, turn, 0)
        if half == 0:
            idx_copy.wait()
        at = pl.ds(first, count)
        for n, o in enumerate(OFFSETS):
            p = peer(o)
            for c in range(slots(o)):
                row = jnp.clip(idx[c, p], 0, POOL - 1) + first * STEP
                for k in range(5):
                    send[p, c, at, k * 128 : (k + 1) * 128] = pf[k, pl.ds(row, count, stride=STEP), :].astype(bf16)
            held_slots = pl.ds(0, slots(o))
            copy = pltpu.make_async_remote_copy(
                src_ref=send.at[p, held_slots, at], dst_ref=recv.at[me, held_slots, at],
                send_sem=page_ss.at[half, n], recv_sem=page_rs.at[half, n], device_id={"req": p}, device_id_type=MESH,
            )
            copy.start()
            copies.append(copy)
    ag_step(1)

    def home_page(e, carry):
        slot = idx[2, e]
        for k in range(5):
            xh[e // KEEP, pl.ds(pl.multiple_of(e % KEEP * ROWS, ROWS), ROWS), k * 128 : (k + 1) * 128] = page_tile(slot, k)
        return carry

    lax.fori_loop(0, 2 * KEEP, home_page, 0)
    ag_step(2)

    lens0, lens1 = idx[4, 2 * me], idx[4, 2 * me + 1]
    tok = iota((1, 2 * NEW), 1)
    places = jnp.where(tok < NEW, lens0 + tok, lens1 + tok - NEW).astype(f32)
    freq = jnp.exp(iota((HALF, 128), 0).astype(f32) * (-2.0 * LOG_THETA / HD))
    angle = freq * places
    cos_sin[0], cos_sin[1] = jnp.cos(angle), jnp.sin(angle)

    loads[7].wait()

    for i in range(20):
        gb[i * 128 : (i + 1) * 128, :] = jnp.transpose(jnp.broadcast_to(gain_ref[i : i + 1, :], (128, 128)))
    ag_step(3)
    loads[3].wait()
    for i in range(20):
        wot[i * 128 : (i + 1) * 128, :] = jnp.transpose(wo[:, i * 128 : (i + 1) * 128])
    group = iota((GROUPS, 64), 0)
    owed = jnp.zeros((GROUPS, 64), f32)
    for j in range(KEEP, KEEP + TAIL):
        owed += ((plan_ref[j : j + 1, :] == group) & (lens_ref[...] > j * PAGE)).astype(f32)
    owed = mm(owed, (iota((64, GROUPS), 0) // 2 == iota((64, GROUPS), 1)).astype(f32), ((1,), (0,)))
    g0, g1 = iota((GROUPS, GROUPS), 0), iota((GROUPS, GROUPS), 1)
    owed = jnp.where(g0 == (g1 + GROUPS // 2) % GROUPS, 0.0, owed)
    more_ref[0] = (jnp.max(owed) > 1.5).astype(jnp.int32)

    loads[2].wait()
    for piece in range(PIECES):
        ags[3, int(not crosses(0, piece)), piece].wait_recv()

    xw = xf[...].astype(f32)
    rstd = lax.rsqrt(jnp.sum(xw * xw, axis=0, keepdims=True) * (1.0 / D) + EPSILON)
    normed = (xw * rstd * gb[...]).astype(bf16)
    proj = mm(w[...], normed, ((1,), (0,)))
    cos, sin = cos_sin[0], cos_sin[1]

    def rotated(first):
        front, back = proj[first : first + HALF], proj[first + HALF : first + HD]
        full = jnp.concatenate([front * cos - back * sin, back * cos + front * sin], axis=0)
        return full.astype(bf16)

    def turned(values):
        padded = jnp.concatenate([values.astype(f32), jnp.zeros((128 - HD, 2 * NEW), f32)], axis=0)
        return jnp.transpose(padded).astype(bf16)

    feature, at_lane = iota((HD, QUERY_LANES), 0), iota((HD, QUERY_LANES), 1)
    spread = feature == at_lane
    for _, _, _, stand in KEY_TILE[1:]:
        spread = spread | (feature == at_lane - stand)
    spread = spread.astype(f32).astype(bf16)
    for g in range(G):
        qt = mm(rotated(g * HD), spread, ((0,), (0,))).astype(bf16)
        for a in range(2):
            qs[a, g * NEW : (g + 1) * NEW, :] = qt[a * NEW : (a + 1) * NEW]
    kn[...] = turned(rotated(G * HD))
    vn[...] = turned(proj[(G + 1) * HD :].astype(bf16))

    t_col = iota((G * NEW, 1), 0) % NEW

    def attend(a, keys, first_pos, top0, with_window):
        length = idx[4, 2 * me + a]
        cols = iota((1, 512), 1)
        top = top0
        for m, (first, width, at, _) in enumerate(KEY_TILE):
            s = mm(qs[a, :, at : at + width], keys[:, first : first + width], ((1,), (1,)))
            rel = cols * 4 + (first_pos + m) - length
            ok = rel < 0
            if with_window:
                ok = ok & (rel > t_col - WINDOW)
            s = jnp.where(ok, s, MASKED)
            sc[m] = s
            top = jnp.maximum(top, jnp.max(s, axis=1, keepdims=True))
        total = jnp.zeros((G * NEW, 1), f32)
        sums = jnp.zeros((G * NEW, 128), f32)
        for m, (first, width, offset) in enumerate(VAL_TILE):
            p = jnp.exp2((sc[m] - top) * SCALE)
            total = total + jnp.sum(p, axis=1, keepdims=True)
            o = mm(p.astype(bf16), keys[:, first : first + width], ((1,), (0,)))
            sums = sums + pltpu.roll(o, width - offset, 1)[:, :128]
        return top, total, sums

    def home(a, carry):
        at = pl.ds(pl.multiple_of(a * NEW, NEW), NEW)
        s = mm(qs[a, :, :128], kn[at, :], ((1,), (1,)))
        s = jnp.where(iota((G * NEW, NEW), 1) <= t_col, s, MASKED)
        top_new = jnp.max(s, axis=1, keepdims=True)
        top, total, sums = attend(a, xh.at[a], 0, top_new, True)
        p = jnp.exp2((s - top) * SCALE)
        stat[a, 0] = jnp.broadcast_to(top, (G * NEW, 128))
        stat[a, 1] = jnp.broadcast_to(total + jnp.sum(p, axis=1, keepdims=True), (G * NEW, 128))
        acc[a] = sums + mm(p.astype(bf16), vn[at, :], ((1,), (0,)))
        return carry

    lax.fori_loop(0, 2, home, 0)

    for copy in copies:
        copy.wait_recv()

    def tail(a, carry):
        for j in range(TAIL):
            where = jnp.clip(idx[3, a * TAIL + j], 0, 2 * GROUPS - 1)
            xt[j * ROWS : (j + 1) * ROWS, :] = recv[where // 2, where % 2]
        old_top = stat[a, 0][:, :1]
        top, total, sums = attend(a, xt, KEEP * PAGE, old_top, False)
        weight = jnp.exp2((old_top - top) * SCALE)
        result = (acc[a] * weight + sums) / (stat[a, 1][:, :1] * weight + total)
        for g in range(G):
            hs[g, pl.ds(pl.multiple_of(a * NEW, NEW), NEW), :] = result[g * NEW : (g + 1) * NEW]
        return carry

    lax.fori_loop(0, 2, tail, 0)
    for g in range(G):
        ht[g * HD : (g + 1) * HD, :] = jnp.transpose(hs[g])[:HD].astype(bf16)

    def project(k):
        rows = pl.ds(pl.multiple_of(lax.rem(z + k, TP) * XB, 64), XB)
        return mm(wot[rows, :], ht[...], ((1,), (0,)))

    size = XB // PIECES
    sums = {}
    for hop in range(4):
        if hop < 2:
            for k in ((4,), (3, 5, 2, 6, 1, 7, 0))[hop]:
                mine[k] = project(k)
        for piece in range(PIECES):
            for way in range(2):
                if hop == 0 and not crosses(way, piece):
                    continue
                n = (hop * 2 + way) * PIECES + piece
                block = mine[4 - hop if way == 0 else 4 + hop, piece * size : (piece + 1) * size, :]
                if (hop - 1, way, piece) in sums:
                    sums[hop - 1, way, piece].wait_recv()
                    block = block + rrecv[n - 2 * PIECES].astype(f32)
                part[n] = block.astype(bf16)
                copy = pltpu.make_async_remote_copy(
                    src_ref=part.at[n], dst_ref=rrecv.at[n], send_sem=rs_ss.at[n], recv_sem=rs_rs.at[n],
                    device_id={"tp": ring[way]}, device_id_type=MESH,
                )
                copy.start()
                sums[hop, way, piece] = copy
    for piece in range(PIECES):
        block = mine[0, piece * size : (piece + 1) * size, :]
        for way in range(2):
            sums[3, way, piece].wait_recv()
            block = block + rrecv[(6 + way) * PIECES + piece].astype(f32)
        out_ref[piece * size : (piece + 1) * size, :] = block

    for copy in list(ags.values()) + copies + list(sums.values()):
        copy.wait_send()


def layer(rounds, *operands):
    any_space = pl.BlockSpec(memory_space=pl.ANY)
    vmem = pl.BlockSpec(memory_space=pltpu.VMEM)
    smem = pl.BlockSpec(memory_space=pltpu.SMEM)
    f32, bf16 = jnp.float32, jnp.bfloat16
    dma = pltpu.SemaphoreType.DMA
    return pl.pallas_call(
        functools.partial(kernel, rounds),
        out_shape=(pltpu.VMEM((XB, 128), f32), jax.ShapeDtypeStruct((1,), jnp.int32)),
        in_specs=[any_space] * 8,
        out_specs=(vmem, smem),
        scratch_shapes=[
            pltpu.VMEM((20, 128), f32),
            pltpu.VMEM((32, 64), jnp.int32),
            pltpu.VMEM((32, 64), jnp.int32),
            pltpu.VMEM((1, 64), jnp.int32),
            pltpu.VMEM((2, HALF, 128), f32),
            pltpu.VMEM((D, 128), bf16),
            pltpu.VMEM((POOL, ROWS * WIDTH), bf16),
            pltpu.VMEM((480, D), bf16),
            pltpu.VMEM((D, 128), f32),
            pltpu.VMEM((XB, D), bf16),
            pltpu.VMEM((D, XB), bf16),
            pltpu.VMEM((5, ROWS * STEP + 8, 128), f32),
            pltpu.VMEM((GROUPS, 2, ROWS, WIDTH), bf16),
            pltpu.VMEM((GROUPS, 2, ROWS, WIDTH), bf16),
            pltpu.VMEM((2, 512, WIDTH), bf16),
            pltpu.VMEM((512, WIDTH), bf16),
            pltpu.VMEM((2, G * NEW, QUERY_LANES), bf16),
            pltpu.VMEM((128, 128), bf16),
            pltpu.VMEM((128, 128), bf16),
            pltpu.VMEM((4, G * NEW, 512), f32),
            pltpu.VMEM((2, 2, G * NEW, 128), f32),
            pltpu.VMEM((2, G * NEW, 128), f32),
            pltpu.VMEM((G, 128, 128), f32),
            pltpu.VMEM((XB, 128), bf16),
            pltpu.VMEM((TP, XB, 128), f32),
            pltpu.VMEM((8 * PIECES, XB // PIECES, 128), bf16),
            pltpu.VMEM((8 * PIECES, XB // PIECES, 128), bf16),
            pltpu.VMEM((8, 128), jnp.int32),
            pltpu.SMEM((8, 128), jnp.int32),
            dma((10,)), dma((2, 31)), dma((2, 31)), *[dma((8 * PIECES,))] * 4,
        ],
        compiler_params=pltpu.CompilerParams(
            collective_id=rounds, has_side_effects=True, vmem_limit_bytes=60 * 2**20
        ),
        name=f"paged_prefill_{rounds}",
    )(*operands)


def local(activations, norm_gain, input_proj, output_proj, cache_pool, page_table, rebalance_plan, cached_lengths, token_positions):
    operands = (
        activations.T,
        norm_gain.reshape(20, 128),
        jnp.transpose(input_proj, (1, 2, 0)).reshape(480, D),
        output_proj,
        cache_pool.reshape(POOL, ROWS * WIDTH),
        page_table.T,
        rebalance_plan.T,
        cached_lengths.reshape(1, 64),
    )
    out, more = layer(1, *operands)
    out = lax.cond(more[0] > 0, lambda first, *rest: layer(2, *rest)[0], lambda first, *rest: first, out, *operands)
    return out.T


def solution(mesh):
    in_specs = (
        P("req", "tp"), P(), P(None, "tp", None), P("tp", None), P("req", "tp", None), P(), P(), P(), P(),
    )
    return jax.shard_map(local, mesh=mesh, in_specs=in_specs, out_specs=P("req", "tp"), check_vma=False)
```
